256 devices in a mesh: row: 32 (over x_lo, z, core), col: 8 (over y, x_hi).
Axes of the slice: x: 4 (x_hi: 2, x_lo: 2; x = x_hi * 2 + x_lo), y: 4, z: 8, core: 2. Of those that a mesh axis runs over, the one named last changes fastest.
Arguments:
- hessian: float32 [14336, 14336], P('row', 'col'), may hold values from -1 to 6, as said below
- dense_weight: float32 [14336, 1024], P('col', 'row'), may hold values from -6 to 6
- start_iterate: float32 [14336, 1024], P('col', 'row'), may hold values from -6 to 6
- start_multiplier: float32 [14336, 1024], P('col', 'row'), may hold values from -3 to 3
- keep_mask: int32 [14336, 1024], P('col', 'row'), may hold values 0 or 1
Outputs:
- iterate: float32 [14336, 1024], P('col', 'row')
- projected: float32 [14336, 1024], P('col', 'row')
- multiplier: float32 [14336, 1024], P('col', 'row')
The draws below stay inside these ranges and needn't reach their ends.
Inputs may be any that keep to these rules, and one draw needn't show every extreme that they name: `hessian`: a calibration Hessian: symmetric up to rounding and positive definite.
All inputs are finite; a program needn't handle non-finite values. No bound on the sum of `keep_mask` on one device may be relied on, other than what follows from the above.
Results may differ from the reference program's by a relative error of at most 0.0001.
Values sent between devices are 32-bit elements; how exact they have to be, the bound alone decides.
A program may use at most 64 MiB of HBM per device.

```python
import math
import jax
import jax.numpy as jnp
from jax import lax

K = 14336
R = 1024
ITERS = 2


def draw_hessian(key, part):
    key_off = jax.random.fold_in(key, 11)
    key_diag = jax.random.fold_in(key, 12)
    key_scale = jax.random.fold_in(key, 13)
    base = jax.random.normal(key_off, (K, K), jnp.float32)
    scales = jnp.exp(jax.random.uniform(key_scale, (K,), jnp.float32, math.log(0.7), math.log(1.4)))
    offdiag = (base + base.T) * (0.25 / math.sqrt(K))
    diagonal = jax.random.uniform(key_diag, (K,), jnp.float32, 1.0, 2.0)
    places = jnp.arange(K)
    core = offdiag.at[places, places].set(diagonal)
    return scales[:, None] * core * scales[None, :]


def set_ends(drawn, key, low, top_value):
    longest = drawn.shape.index(max(drawn.shape))
    spots = []
    for shift in (0, 1):
        where = [jax.random.randint(jax.random.fold_in(key, axis), (), 0, length) for axis, length in enumerate(drawn.shape)]
        where[longest] = (where[longest] + shift) % drawn.shape[longest]
        spots.append(tuple(where))
    return drawn.at[spots[0]].set(low).at[spots[1]].set(top_value)


def levels(key, dims, pieces, smallest, high):
    loudness = 1.0
    for axis_at, blocks in pieces:
        draws = jax.random.uniform(jax.random.fold_in(jax.random.fold_in(key, 6), axis_at), (blocks,), jnp.float32, smallest / len(pieces), high / len(pieces))
        loudness = loudness * jnp.repeat(jnp.exp(draws), dims[axis_at] // blocks).reshape((-1,) + (1,) * (len(dims) - 1 - axis_at))
    return loudness


def gaussian(rng, extent, spread, limit, cuts=(), kind=jnp.bfloat16):
    gain = levels(rng, extent, cuts, -0.22, 0.18) if cuts else 1.0
    result = jax.random.normal(rng, extent, jnp.float32) * spread * gain
    return jnp.minimum(jnp.maximum(result, -limit), limit).astype(kind)


def setup_inputs(seed: int = 0) -> dict:
    key_of = jax.random.split(jax.random.key(seed), 6)
    hessian = draw_hessian(jax.random.fold_in(key_of[5], 71), 0)
    dense_weight = gaussian(key_of[1], (K, R), 1.0, 6.0, ((0, 8), (1, 32)), jnp.float32)
    start_iterate = gaussian(key_of[2], (K, R), 1.0, 6.0, ((0, 8), (1, 32)), jnp.float32)
    start_multiplier = gaussian(key_of[3], (K, R), 0.5, 3.0, ((0, 8), (1, 32)), jnp.float32)
    keep_mask = set_ends((jax.random.randint(key_of[4], (K, R), 0, 2) < 1).astype(jnp.int32), jax.random.fold_in(key_of[4], 1), 0, 1)
    return {"hessian": hessian, "dense_weight": dense_weight, "start_iterate": start_iterate, "start_multiplier": start_multiplier, "keep_mask": keep_mask}


step_size = 0.25
penalty = 1.0


def reference(hessian, dense_weight, start_iterate, start_multiplier, keep_mask):
    keeping = keep_mask.astype(jnp.float32)
    iterate = start_iterate
    multiplier = start_multiplier
    projected = keeping * (iterate + multiplier)
    for rounds in range(ITERS):
        change = iterate - dense_weight
        gradient = jnp.dot(hessian, change, precision=lax.Precision.HIGHEST, preferred_element_type=jnp.float32)
        iterate = iterate - step_size * (gradient + penalty * (iterate - projected + multiplier))
        projected = keeping * (iterate + multiplier)
        multiplier = multiplier + iterate - projected
    return iterate, projected, multiplier
```

```python
import jax
import jax.numpy as jnp
from jax import lax
from jax.experimental import pallas as pl
from jax.experimental.pallas import tpu as pltpu
from jax.sharding import PartitionSpec as P

MESH = pl.DeviceIdType.MESH
STEP = 0.25
U = 4
KC = 1792
KR = 896
F32 = jnp.float32
BF16 = jnp.bfloat16


def make_schedule():
    items = []
    gap, hop = 6.4, 2.0
    for u in range(U):
        t = u * gap
        for s in range(6):
            items.append((t + s * hop, u, "ag", s))
        t += 5 * hop + 0.1
        items.append((t, u, "mm", 0))
        t += 5.0
        items.append((t, u, "rsy2", 0))
        t += 3.5
        items.append((t, u, "xhi", 0))
        t += 4.5
        items.append((t, u, "agy1", 0))
        t += 3.5
        items.append((t, u, "agy2", 0))
        t += 4.0
        items.append((t, u, "mmt", 0))
        t += 2.5
        for s in range(1, 6):
            items.append((t + s * hop, u, "rs", s))
    return sorted(items)


SCHEDULE = make_schedule()


def kernel(
    h_ref, c0_ref, a_ref, c1_out, g1_out,
    hbuf, hhi, hlo, xs_ref, xall, pbuf, rb1, rb2, vbuf, xb, c1all, cs_ref, qbuf,
    rx1, rza, rzb, rpa, rpb, rxf, ab, ch, ss, rs, hs,
):
    row = lax.axis_index("row")
    col = lax.axis_index("col")
    k = row % 2
    z = (row // 2) % 8
    x = row // 16
    y = col // 2
    xh = col % 2
    d = 1 - 2 * k
    xo = 1 - x

    def zi(off):
        return (z + d * off + 16) % 8

    def dev_z(off):
        return (x * 16 + zi(off) * 2 + k, col)

    dev_a, dev_b = dev_z(1), dev_z(-1)
    dev_x = (xo * 16 + z * 2 + k, col)
    dev_core = (x * 16 + z * 2 + (1 - k), col)
    y1 = y + 1 - 2 * (y % 2)
    y3 = 3 - y
    dev_y1 = (row, y1 * 2 + xh)
    dev_y3 = (row, y3 * 2 + xh)
    dev_xh = (row, y * 2 + (1 - xh))

    b0, b1 = y % 2, y // 2
    bx = (b0 + b1) % 2
    f1 = (bx, b1)
    f2 = (1 - b1, 1 - b0)
    q = (2 * f1[0] + f2[0], 2 * f1[1] + f2[1])

    cblk = y * 2 + xh
    qz = z // 2
    e0, e1 = qz % 2, qz // 2
    ya_b1 = 1 - e0
    ya_b0 = (e1 + ya_b1) % 2
    y_if0 = 2 * ya_b1 + ya_b0
    y_if1 = 2 * e1 + (1 - e0)
    yd = (1 - x) * y_if0 + x * y_if1
    dev_out = []
    for h in range(2):
        r = 2 * cblk + h
        dev_out.append(((r // 8) * 16 + (r % 8) * 2 + k, yd * 2 + x))
    rblk = x * 8 + z
    qh = (1 - xh) * q[0] + xh * q[1]
    dev_in = [(xh * 16 + (2 * qh + i) * 2 + k, rblk // 2) for i in range(2)]
    hpart = rblk % 2

    barrier = pltpu.get_barrier_semaphore()
    peers = [dev_a, dev_b, dev_x, dev_core, dev_y1, dev_y3, dev_xh] + dev_out + dev_in
    for p in peers:
        pl.semaphore_signal(barrier, inc=1, device_id=p, device_id_type=MESH)
    pl.semaphore_wait(barrier, len(peers))

    names = {}
    sends = []

    def sem(name):
        return names.setdefault(name, len(names))

    def send(name, src, dst, dev):
        i = sem(name)
        c = pltpu.make_async_remote_copy(
            src_ref=src, dst_ref=dst, send_sem=ss.at[i], recv_sem=rs.at[i],
            device_id=dev, device_id_type=MESH,
        )
        c.start()
        sends.append(c)

    def wait(name, slot):
        i = sem(name)
        pltpu.make_async_remote_copy(
            src_ref=slot, dst_ref=slot, send_sem=ss.at[i], recv_sem=rs.at[i],
            device_id=dev_x, device_id_type=MESH,
        ).wait_recv()

    LO = pl.ds(0, KR)
    HI = pl.ds(KR, KR)

    hcopy = pltpu.make_async_copy(h_ref, hbuf.at[k], hs.at[0])

    def start_h():
        hcopy.start()
        send("h", h_ref, hbuf.at[k], dev_core)

    def split_rows(part):
        @pl.loop(0, 28)
        def _(i):
            r0 = pl.multiple_of(i * 16, 16)
            v = hbuf[part, pl.ds(r0, 16), :]
            hi = v.astype(BF16)
            o0 = pl.multiple_of(part * 448 + i * 16, 16)
            hhi[pl.ds(o0, 16), :] = hi
            hlo[pl.ds(o0, 16), :] = (v - hi.astype(F32)).astype(BF16)

    def ag(u, s):
        full = lambda o: xall.at[u, x, zi(o)]
        if s == 0:
            xall[u, x, z] = c0_ref[u]
            send(f"fa{u}.1", c0_ref.at[u], full(0), dev_a)
            send(f"fb{u}.1", c0_ref.at[u], full(0), dev_b)
            send(f"x{u}", c0_ref.at[u], full(0), dev_x)
            return
        par = lambda o: xall.at[u, xo, zi(o), :, HI]
        low = lambda o: xall.at[u, x, zi(o), :, LO]
        if s <= 4:
            wait(f"fa{u}.{s}", full(-s))
            if s < 4:
                send(f"fa{u}.{s + 1}", full(-s), full(-s), dev_a)
        if s <= 3:
            wait(f"fb{u}.{s}", full(s))
            if s < 3:
                send(f"fb{u}.{s + 1}", full(s), full(s), dev_b)
        if s == 1:
            wait(f"x{u}", xall.at[u, xo, z])
            send(f"pa{u}.1", par(0), par(0), dev_a)
            send(f"pb{u}.1", par(0), par(0), dev_b)
        elif s <= 5:
            if s - 1 <= 3:
                wait(f"pa{u}.{s - 1}", par(-(s - 1)))
                if s - 1 < 3:
                    send(f"pa{u}.{s}", par(-(s - 1)), par(-(s - 1)), dev_a)
            wait(f"pb{u}.{s - 1}", par(s - 1))
            if s - 1 < 4:
                send(f"pb{u}.{s}", par(s - 1), par(s - 1), dev_b)
        if s <= 4:
            send(f"xa{u}.{s}", low(-s), low(-s), dev_x)
        if s <= 3:
            send(f"xb{u}.{s}", low(s), low(s), dev_x)
        if s == 5:
            olow = lambda o: xall.at[u, xo, zi(o), :, LO]
            for j in range(1, 5):
                wait(f"xa{u}.{j}", olow(-j))
            for j in range(1, 4):
                wait(f"xb{u}.{j}", olow(j))

    NT = (((1,), (1,)), ((), ()))
    NN = (((1,), (0,)), ((), ()))

    def mm(u):
        for half in range(2):
            split_half(xall, u, half, xs_ref, KC)
        lhs = xs_ref[...]

        def part(c0, n):
            r = lax.dot_general(lhs, hhi[pl.ds(c0, n), :], NT, preferred_element_type=F32)
            r2 = lax.dot_general(lhs[:128], hlo[pl.ds(c0, n), :], NT, preferred_element_type=F32)
            v = (r[:128] + r[128:] + r2) * (-STEP)
            return v.reshape(2, 8, 8, n)

        @pl.loop(0, 3)
        def _(j):
            c0 = pl.multiple_of(j * 256, 256)
            pbuf[u, :, :, :, pl.ds(c0, 256)] = part(c0, 256)

        pbuf[u, :, :, :, pl.ds(768, 128)] = part(768, 128)
        send(f"r1{u}.0", pbuf.at[u, 0, pl.ds(4 * (1 - f1[0]), 4)], rb1.at[u, 0], dev_y1)
        send(f"r1{u}.1", pbuf.at[u, 1, pl.ds(4 * (1 - f1[1]), 4)], rb1.at[u, 1], dev_y3)

    def split_half(src, u, half, dst, width):
        @pl.loop(0, 4)
        def _(i):
            v = src[u, half, pl.ds(i * 2, 2)].reshape(16, width)
            hi = v.astype(BF16)
            r0 = half * 64 + i * 16
            dst[pl.ds(pl.multiple_of(r0, 16), 16), :] = hi
            dst[pl.ds(pl.multiple_of(128 + r0, 16), 16), :] = (v - hi.astype(F32)).astype(BF16)

    def rsy2(u):
        for hf, dev2 in ((0, dev_y3), (1, dev_y1)):
            wait(f"r1{u}.{hf}", rb1.at[u, hf])
            base = 4 * f1[hf]
            o = 2 * (1 - f2[hf])
            pbuf[u, hf, pl.ds(base + o, 2)] = pbuf[u, hf, pl.ds(base + o, 2)] + rb1[u, hf, pl.ds(o, 2)]
            send(f"r2{u}.{hf}", pbuf.at[u, hf, pl.ds(base + o, 2)], rb2.at[u, hf], dev2)
        for hf in range(2):
            o = 2 * f2[hf]
            vbuf[u, hf] = pbuf[u, hf, pl.ds(4 * f1[hf] + o, 2)] + rb1[u, hf, pl.ds(o, 2)]
        for i in range(2):
            wait_a(u, i)
        vbuf[u, xh] = vbuf[u, xh] + ab[u]

    def wait_a(u, i):
        n0 = sem(f"a{u}.{i}")
        pltpu.make_async_remote_copy(
            src_ref=ab.at[u, i], dst_ref=ab.at[u, i], send_sem=ss.at[n0], recv_sem=rs.at[n0],
            device_id=dev_x, device_id_type=MESH,
        ).wait_recv()

    def xhi(u):
        for hf in range(2):
            wait(f"r2{u}.{hf}", rb2.at[u, hf])
            vbuf[u, hf] = vbuf[u, hf] + rb2[u, hf]
        send(f"xh{u}", vbuf.at[u], xb.at[u], dev_xh)

    def agy1(u):
        wait(f"xh{u}", xb.at[u])
        for hf, dev in ((0, dev_y3), (1, dev_y1)):
            slot = c1all.at[u, hf, pl.ds(2 * q[hf], 2)]
            c1all[u, hf, pl.ds(2 * q[hf], 2)] = vbuf[u, hf] + xb[u, hf]
            send(f"g1{u}.{hf}", slot, slot, dev)
        for i in range(2):
            send_home(u, i)

    def send_home(u, i):
        src = c1all.at[u, xh, 2 * qh + i]
        n0 = sem(f"c{u}.{i}")
        c = pltpu.make_async_remote_copy(
            src_ref=src, dst_ref=ch.at[u, hpart], send_sem=ss.at[n0],
            recv_sem=rs.at[sem(f"c{u}.0r") + hpart],
            device_id=dev_in[i], device_id_type=MESH,
        )
        c.start()
        sends.append(c)

    def agy2(u):
        for hf, dev, dev2 in ((0, dev_y3, dev_y1), (1, dev_y1, dev_y3)):
            o = 4 * f1[hf] + 2 * (1 - f2[hf])
            wait(f"g1{u}.{hf}", c1all.at[u, hf, pl.ds(o, 2)])
            slot = c1all.at[u, hf, pl.ds(4 * f1[hf], 4)]
            send(f"g2{u}.{hf}", slot, slot, dev2)

    def mmt(u):
        for hf in range(2):
            wait(f"g2{u}.{hf}", c1all.at[u, hf, pl.ds(4 * (1 - f1[hf]), 4)])
        for half in range(2):
            split_half(c1all, u, half, cs_ref, KR)
        lhs = cs_ref[...]

        @pl.loop(0, 7)
        def _(j):
            c0 = pl.multiple_of(j * 256, 256)
            r = lax.dot_general(lhs, hhi[:, pl.ds(c0, 256)], NN, preferred_element_type=F32)
            r2 = lax.dot_general(lhs[:128], hlo[:, pl.ds(c0, 256)], NN, preferred_element_type=F32)
            qbuf[u, :, :, :, pl.ds(c0, 256)] = (r[:128] + r[128:] + r2).reshape(2, 8, 8, 256)

        for o in (4, -3, 3, -2, 2, -1, 1, 0):
            send(f"y{u}.{o}", qbuf.at[u, xo, zi(o), :, LO], rx1.at[u, zi(o)], dev_x)
        hi_of = lambda o: qbuf.at[u, xo, zi(o), :, HI]
        send(f"ha{u}.1", hi_of(3), rpa.at[u, 0], dev_a)
        send(f"hb{u}.1", hi_of(-4), rpb.at[u, 0], dev_b)

    def rsum(u, s):
        def take_x(o):
            wait(f"y{u}.{o}", rx1.at[u, zi(o)])
            qbuf[u, x, zi(o), :, LO] = qbuf[u, x, zi(o), :, LO] + rx1[u, zi(o)]

        def add(o, buf, j):
            qbuf[u, x, zi(o)] = qbuf[u, x, zi(o)] + buf[u, j]

        def addh(o, buf, j):
            qbuf[u, xo, zi(o), :, HI] = qbuf[u, xo, zi(o), :, HI] + buf[u, j]

        if s <= 4:
            o = 5 - s
            take_x(o)
            if s > 1:
                wait(f"za{u}.{s - 1}", rza.at[u, s - 2])
                add(o, rza, s - 2)
            send(f"za{u}.{s}", qbuf.at[u, x, zi(o)], rza.at[u, s - 1], dev_a)
        if s <= 3:
            o = -(4 - s)
            take_x(o)
            if s > 1:
                wait(f"zb{u}.{s - 1}", rzb.at[u, s - 2])
                add(o, rzb, s - 2)
            send(f"zb{u}.{s}", qbuf.at[u, x, zi(o)], rzb.at[u, s - 1], dev_b)
        if s <= 3:
            wait(f"ha{u}.{s}", rpa.at[u, s - 1])
            o = 3 - s
            addh(o, rpa, s - 1)
            if s < 3:
                send(f"ha{u}.{s + 1}", qbuf.at[u, xo, zi(o), :, HI], rpa.at[u, s], dev_a)
        if s <= 4:
            wait(f"hb{u}.{s}", rpb.at[u, s - 1])
            o = -(4 - s)
            addh(o, rpb, s - 1)
            if s < 4:
                send(f"hb{u}.{s + 1}", qbuf.at[u, xo, zi(o), :, HI], rpb.at[u, s], dev_b)
            else:
                send(f"xf{u}", qbuf.at[u, xo, z, :, HI], rxf.at[u], dev_x)
        if s == 5:
            take_x(0)
            wait(f"zb{u}.3", rzb.at[u, 2])
            wait(f"za{u}.4", rza.at[u, 3])
            wait(f"xf{u}", rxf.at[u])
            v = qbuf[u, x, z] + rza[u, 3] + rzb[u, 2]
            g1_out[u, :, LO] = v[:, :KR]
            g1_out[u, :, HI] = v[:, KR:] + rxf[u]
            for h in range(2):
                n0 = sem(f"c{u}.0r") + h
                pltpu.make_async_remote_copy(
                    src_ref=ch.at[u, h], dst_ref=ch.at[u, h], send_sem=ss.at[n0], recv_sem=rs.at[n0],
                    device_id=dev_x, device_id_type=MESH,
                ).wait_recv()
                c1_out[u, :, pl.ds(h * KR, KR)] = ch[u, h]

    for u in range(U):
        for i in range(2):
            sem(f"a{u}.{i}")
        sem(f"c{u}.0r")
        sem(f"c{u}.1r")

    def relay_send(u):
        for h in range(2):
            n0 = sem(f"as{u}.{h}")
            c = pltpu.make_async_remote_copy(
                src_ref=a_ref.at[u, :, pl.ds(h * KR, KR)], dst_ref=ab.at[u, z % 2],
                send_sem=ss.at[n0], recv_sem=rs.at[sem(f"a{u}.0") + z % 2],
                device_id=dev_out[h], device_id_type=MESH,
            )
            c.start()
            sends.append(c)

    start_h()
    for t, u, name, s in SCHEDULE:
        if name == "ag":
            ag(u, s)
            if s == 1:
                relay_send(u)
            if u == 0 and s == 1:
                hcopy.wait()
                split_rows(k)
            if u == 0 and s == 3:
                wait("h", hbuf.at[1 - k])
                split_rows(1 - k)
        elif name == "rs":
            rsum(u, s)
        else:
            {"mm": mm, "rsy2": rsy2, "xhi": xhi, "agy1": agy1, "agy2": agy2, "mmt": mmt}[name](u)
    for c in sends:
        c.wait_send()
    assert len(names) <= NSEM, len(names)


NSEM = 320


def run_kernel(h, c0, a):
    v = pltpu.VMEM
    scratch = [
        v((2, 448, KC), F32), v((KR, KC), BF16), v((KR, KC), BF16), v((256, KC), BF16),
        v((U, 2, 8, 8, KC), F32),
        v((U, 2, 8, 8, KR), F32),
        v((U, 2, 4, 8, KR), F32), v((U, 2, 2, 8, KR), F32),
        v((U, 2, 2, 8, KR), F32), v((U, 2, 2, 8, KR), F32),
        v((U, 2, 8, 8, KR), F32), v((256, KR), BF16),
        v((U, 2, 8, 8, KC), F32),
        v((U, 8, 8, KR), F32),
        v((U, 4, 8, KC), F32), v((U, 3, 8, KC), F32),
        v((U, 3, 8, KR), F32), v((U, 4, 8, KR), F32),
        v((U, 8, KR), F32),
        v((U, 2, 8, KR), F32), v((U, 2, 8, KR), F32),
        pltpu.SemaphoreType.DMA((NSEM,)), pltpu.SemaphoreType.DMA((NSEM,)),
        pltpu.SemaphoreType.DMA((1,)),
    ]
    return pl.pallas_call(
        kernel,
        out_shape=[jax.ShapeDtypeStruct((U, 8, KC), F32)] * 2,
        in_specs=[pl.BlockSpec(memory_space=pl.ANY)] + [pl.BlockSpec(memory_space=pltpu.VMEM)] * 2,
        out_specs=[pl.BlockSpec(memory_space=pltpu.VMEM)] * 2,
        scratch_shapes=scratch,
        compiler_params=pltpu.CompilerParams(
            collective_id=0, has_side_effects=True, vmem_limit_bytes=56 * 1024 * 1024
        ),
    )(h, c0, a)


def per_device(hessian, dense_weight, start_iterate, start_multiplier, keep_mask):
    weight, iterate0, multiplier0 = dense_weight.T, start_iterate.T, start_multiplier.T
    keeping = keep_mask.T.astype(F32)
    projected0 = keeping * (iterate0 + multiplier0)
    change = iterate0 - weight
    start = change - STEP * (iterate0 - projected0 + multiplier0)
    c1, g1 = run_kernel(hessian, change.reshape(U, 8, KC), start.reshape(U, 8, KC))
    iterate1 = c1.reshape(32, KC) + weight
    projected1 = keeping * (iterate1 + multiplier0)
    multiplier1 = multiplier0 + iterate1 - projected1
    iterate2 = iterate1 - STEP * (g1.reshape(32, KC) + (iterate1 - projected1 + multiplier1))
    projected2 = keeping * (iterate2 + multiplier1)
    multiplier2 = multiplier1 + iterate2 - projected2
    return iterate2.T, projected2.T, multiplier2.T


def solution(mesh):
    return jax.shard_map(
        per_device,
        mesh=mesh,
        in_specs=(P("row", "col"),) + (P("col", "row"),) * 4,
        out_specs=(P("col", "row"),) * 3,
        check_vma=False,
    )
```

```python
import jax
import jax.numpy as jnp
from jax import lax
from jax.experimental import pallas as pl
from jax.experimental.pallas import tpu as pltpu
from jax.sharding import PartitionSpec as P

MESH = pl.DeviceIdType.MESH
STEP = 0.25
U = 4
KC = 1792
KR = 896
F32 = jnp.float32
BF16 = jnp.bfloat16


ORDER = (
    ("ag0", 1, 0), ("ag0", 2, 0), ("ag0", 3, 0), ("gx", 0, 0), ("rel", 0, 0), ("ga", 0, 1), ("gb", 0, 1),
    ("gx", 1, 0), ("rel", 1, 0), ("gb", 1, 1), ("ga", 1, 1), ("gx", 2, 0), ("rel", 2, 0), ("ga", 2, 1),
    ("gb", 2, 1), ("gx", 3, 0), ("rel", 3, 0), ("gb", 3, 1), ("ga", 3, 1), ("gpb", 0, 1), ("gpa", 0, 1),
    ("gb", 0, 2), ("ga", 0, 2), ("gpa", 1, 1), ("gpb", 1, 1), ("ga", 1, 2), ("gb", 1, 2), ("gpb", 2, 1),
    ("gpa", 2, 1), ("ga", 2, 2), ("gb", 2, 2), ("gpb", 3, 1), ("gpa", 3, 1), ("ga", 3, 2), ("gb", 3, 2),
    ("gpa", 0, 2), ("gpb", 0, 2), ("ga", 0, 3), ("gb", 0, 3), ("gpb", 1, 2), ("gpa", 1, 2), ("ga", 1, 3),
    ("gb", 1, 3), ("gpb", 2, 2), ("gpa", 2, 2), ("gb", 2, 3), ("ga", 2, 3), ("gpb", 3, 2), ("gpa", 3, 2),
    ("ga", 3, 3), ("gb", 3, 3), ("rel2", 0, 0), ("rel2", 1, 0), ("gpb", 0, 3), ("rel2", 2, 0), ("rel2", 3, 0),
    ("gpb", 1, 3), ("ga", 0, 4), ("gpb", 2, 3), ("gpb", 3, 3), ("ga", 1, 4), ("mm", 0, 0), ("ga", 2, 4),
    ("ga", 3, 4), ("mm", 0, 1), ("mm", 1, 0), ("mm", 1, 1), ("mm", 2, 0), ("ry", 0, 0), ("ry", 0, 1),
    ("mm", 2, 1), ("mm", 3, 0), ("ry", 1, 1), ("ry", 1, 0), ("xhi", 0, 0), ("mm", 3, 1), ("ry", 2, 1),
    ("ry", 2, 0), ("xhi", 1, 0), ("ay1", 0, 0), ("ry", 3, 1), ("ry", 3, 0), ("xhi", 2, 0), ("ay2", 0, 0),
    ("ay2", 0, 1), ("ay1", 1, 0), ("xhi", 3, 0), ("crel", 0, 0), ("ay1", 2, 0), ("mmt", 0, 0), ("ay2", 1, 1),
    ("ay2", 1, 0), ("crel", 1, 0), ("ay1", 3, 0), ("ay2", 2, 0), ("ay2", 2, 1), ("mmt", 0, 1), ("ra", 0, 1),
    ("rb", 0, 1), ("crel", 2, 0), ("mmt", 1, 0), ("rpa", 0, 1), ("rpb", 0, 1), ("ra", 0, 2), ("rb", 0, 2),
    ("ay2", 3, 0), ("ay2", 3, 1), ("crel", 3, 0), ("mmt", 1, 1), ("ra", 1, 1), ("mmt", 2, 0), ("rpa", 0, 2),
    ("rpb", 0, 2), ("ra", 0, 3), ("rb", 0, 3), ("rb", 1, 1), ("rpa", 1, 1), ("rpb", 1, 1), ("mmt", 2, 1),
    ("ra", 1, 2), ("mmt", 3, 0), ("rpb", 0, 3), ("ra", 0, 4), ("ra", 2, 1), ("rpa", 1, 2), ("rb", 2, 1),
    ("rpa", 2, 1), ("rb", 1, 2), ("mmt", 3, 1), ("rpb", 1, 2), ("rpf", 0, 0), ("ra", 1, 3), ("rpb", 2, 1),
    ("ra", 3, 1), ("rb", 3, 1), ("rb", 2, 2), ("ra", 2, 2), ("rb", 1, 3), ("rpa", 2, 2), ("rpb", 3, 1),
    ("rpb", 1, 3), ("rpa", 3, 1), ("rpb", 2, 2), ("fin", 0, 0), ("ra", 1, 4), ("rb", 3, 2), ("ra", 3, 2),
    ("rb", 2, 3), ("ra", 2, 3), ("rpa", 3, 2), ("rpb", 3, 2), ("rpf", 1, 0), ("rpb", 2, 3), ("ra", 3, 3),
    ("rb", 3, 3), ("fin", 1, 0), ("ra", 2, 4), ("rpb", 3, 3), ("rpf", 2, 0), ("ra", 3, 4), ("fin", 2, 0),
    ("rpf", 3, 0), ("fin", 3, 0),
)


def kernel(
    h_ref, w_ref, i_ref, m_ref, k_ref, c1_out, g1_out,
    wv, iv, mv, kv, c0_ref, a_ref,
    hbuf, hhi, hlo, xs_ref, xall, pbuf, rb1, rb2, vbuf, xb, c1all, cs_ref, qbuf,
    rx1, rza, rzb, rpa, rpb, rxf, ab, ch, ai, ci, ss, rs, hs,
):
    row = lax.axis_index("row")
    col = lax.axis_index("col")
    k = row % 2
    z = (row // 2) % 8
    x = row // 16
    y = col // 2
    xh = col % 2
    d = 1 - 2 * k
    xo = 1 - x

    def zi(off):
        return (z + d * off + 16) % 8

    def dev_z(off):
        return (x * 16 + zi(off) * 2 + k, col)

    dev_a, dev_b = dev_z(1), dev_z(-1)
    dev_x = (xo * 16 + z * 2 + k, col)
    dev_core = (x * 16 + z * 2 + (1 - k), col)
    y1 = y + 1 - 2 * (y % 2)
    y3 = 3 - y
    dev_y1 = (row, y1 * 2 + xh)
    dev_y3 = (row, y3 * 2 + xh)
    dev_xh = (row, y * 2 + (1 - xh))

    b0, b1 = y % 2, y // 2
    bx = (b0 + b1) % 2
    m0, m1 = (z // 2) % 2, z // 4
    f1 = ((bx + m1) % 2, (b1 + m1) % 2)
    f2 = ((1 - b1 + m0) % 2, (1 - b0 + m0) % 2)
    q = (2 * f1[0] + f2[0], 2 * f1[1] + f2[1])
    q0 = (2 * bx + 1 - b1, 2 * b1 + 1 - b0)

    cblk = y * 2 + xh
    e0, e1 = (z // 2 + cblk) % 2, (z // 4 + (cblk % 4) // 2) % 2
    ya_b1 = 1 - e0
    ya_b0 = (e1 + ya_b1) % 2
    y_if0 = 2 * ya_b1 + ya_b0
    y_if1 = 2 * e1 + (1 - e0)
    yd = (1 - x) * y_if0 + x * y_if1
    md = 2 * ((q0[1] // 2) * xh + (q0[0] // 2) * (1 - xh) + z // 4 - 2 * (((q0[1] // 2) * xh + (q0[0] // 2) * (1 - xh)) * (z // 4)))
    t0 = (q0[1] % 2) * xh + (q0[0] % 2) * (1 - xh)
    md = md + t0 + (z // 2) % 2 - 2 * (t0 * ((z // 2) % 2))
    dev_mid = ((y // 2) * 16 + z * 2 + k, yd * 2 + x)
    dev_home = (xh * 16 + z * 2 + k, 4 * x + md)
    dev_zz = [(x * 16 + (2 * md + h) * 2 + k, col) for h in range(2)]

    def here(dev):
        return jnp.logical_and(dev[0] == row, dev[1] == col)

    hpart = z % 2

    barrier = pltpu.get_barrier_semaphore()
    peers = [dev_a, dev_b, dev_x, dev_core, dev_y1, dev_y3, dev_xh]
    for p in peers:
        pl.semaphore_signal(barrier, inc=1, device_id=p, device_id_type=MESH)
    expected = len(peers)
    for p in [dev_mid, dev_home] + dev_zz:
        same = here(p)
        expected = expected + 1 - same.astype(jnp.int32)

        @pl.when(jnp.logical_not(same))
        def _():
            pl.semaphore_signal(barrier, inc=1, device_id=p, device_id_type=MESH)

    loads = [
        pltpu.make_async_copy(src, dst, hs.at[n])
        for n, (src, dst) in enumerate(((w_ref, wv), (i_ref, iv), (m_ref, mv), (k_ref, kv), (h_ref, hbuf.at[k])))
    ]
    for c in loads:
        c.start()
    loads[0].wait()
    loads[1].wait()
    for u in range(U):
        c0_ref[u] = iv[u] - wv[u]
    loads[2].wait()
    loads[3].wait()
    for u in range(U):
        v0, m0 = iv[u], mv[u]
        p0 = kv[u].astype(F32) * (v0 + m0)
        a_ref[u] = c0_ref[u] - STEP * (v0 - p0 + m0)
        xall[u, x, z] = c0_ref[u]

    names = {}
    sends = []
    moves = []

    def sem(name):
        return names.setdefault(name, len(names))

    def send(name, src, dst, dev):
        i = sem(name)
        c = pltpu.make_async_remote_copy(
            src_ref=src, dst_ref=dst, send_sem=ss.at[i], recv_sem=rs.at[i],
            device_id=dev, device_id_type=MESH,
        )
        c.start()
        sends.append(c)

    def move(name, recv, src, dst, dev):
        i = sem(name)
        same = here(dev)
        c = pltpu.make_async_remote_copy(
            src_ref=src, dst_ref=dst, send_sem=ss.at[i], recv_sem=rs.at[recv],
            device_id=dev, device_id_type=MESH,
        )

        @pl.when(jnp.logical_not(same))
        def _():
            c.start()

        @pl.when(same)
        def _():
            pltpu.make_async_copy(src, dst, rs.at[recv]).start()

        moves.append((c, same))

    def wait(name, slot):
        i = sem(name)
        pltpu.make_async_remote_copy(
            src_ref=slot, dst_ref=slot, send_sem=ss.at[i], recv_sem=rs.at[i],
            device_id=dev_x, device_id_type=MESH,
        ).wait_recv()

    LO = pl.ds(0, KR)
    HI = pl.ds(KR, KR)

    def split_rows(part):
        @pl.loop(0, 28)
        def _(i):
            r0 = pl.multiple_of(i * 16, 16)
            v = hbuf[part, pl.ds(r0, 16), :]
            hi = v.astype(BF16)
            o0 = pl.multiple_of(part * 448 + i * 16, 16)
            hhi[pl.ds(o0, 16), :] = hi
            hlo[pl.ds(o0, 16), :] = (v - hi.astype(F32)).astype(BF16)

    def full(u, o):
        return xall.at[u, x, zi(o)]

    def par(u, o):
        return xall.at[u, xo, zi(o), :, HI]

    def low(u, o):
        return xall.at[u, x, zi(o), :, LO]

    def ag0(u, s):
        send(f"fa{u}.1", c0_ref.at[u], full(u, 0), dev_a)
        send(f"fb{u}.1", c0_ref.at[u], full(u, 0), dev_b)
        send(f"x{u}", c0_ref.at[u], full(u, 0), dev_x)

    def ga(u, s):
        wait(f"fa{u}.{s}", full(u, -s))
        if s < 4:
            send(f"fa{u}.{s + 1}", full(u, -s), full(u, -s), dev_a)
        send(f"xa{u}.{s}", low(u, -s), low(u, -s), dev_x)

    def gb(u, s):
        wait(f"fb{u}.{s}", full(u, s))
        if s < 3:
            send(f"fb{u}.{s + 1}", full(u, s), full(u, s), dev_b)
        send(f"xb{u}.{s}", low(u, s), low(u, s), dev_x)

    def gx(u, s):
        wait(f"x{u}", xall.at[u, xo, z])
        send(f"pa{u}.1", par(u, 0), par(u, 0), dev_a)
        send(f"pb{u}.1", par(u, 0), par(u, 0), dev_b)

    def gpa(u, s):
        wait(f"pa{u}.{s}", par(u, -s))
        send(f"pa{u}.{s + 1}", par(u, -s), par(u, -s), dev_a)

    def gpb(u, s):
        wait(f"pb{u}.{s}", par(u, s))
        send(f"pb{u}.{s + 1}", par(u, s), par(u, s), dev_b)

    def wait_gather(u):
        wait(f"pa{u}.3", par(u, -3))
        wait(f"pb{u}.4", par(u, 4))
        olow = lambda o: xall.at[u, xo, zi(o), :, LO]
        for j in range(1, 5):
            wait(f"xa{u}.{j}", olow(-j))
        for j in range(1, 4):
            wait(f"xb{u}.{j}", olow(j))

    NT = (((1,), (1,)), ((), ()))
    NN = (((1,), (0,)), ((), ()))

    def mm_part(u, c0, n):
        r = lax.dot_general(xs_ref[...], hhi[pl.ds(c0, n), :], NT, preferred_element_type=F32)
        r2 = lax.dot_general(xs_ref[:128], hlo[pl.ds(c0, n), :], NT, preferred_element_type=F32)
        v = (r[:128] + r[128:] + r2) * (-STEP)
        pbuf[u, :, :, :, pl.ds(c0, n)] = v.reshape(2, 8, 8, n)

    def mm(u, s):
        if s == 0:
            wait_gather(u)
            if u == 0:
                wait("h", hbuf.at[1 - k])
                split_rows(1 - k)
            for half in range(2):
                split_half(xall, u, half, xs_ref, KC)

            @pl.loop(0, 2)
            def _(j):
                mm_part(u, pl.multiple_of(j * 256, 256), 256)

            return
        mm_part(u, 512, 256)
        mm_part(u, 768, 128)
        send(f"r1{u}.0", pbuf.at[u, 0, pl.ds(4 * (1 - f1[0]), 4)], rb1.at[u, 0], dev_y1)
        send(f"r1{u}.1", pbuf.at[u, 1, pl.ds(4 * (1 - f1[1]), 4)], rb1.at[u, 1], dev_y3)

    def split_half(src, u, half, dst, width):
        @pl.loop(0, 4)
        def _(i):
            v = src[u, half, pl.ds(i * 2, 2)].reshape(16, width)
            hi = v.astype(BF16)
            r0 = half * 64 + i * 16
            dst[pl.ds(pl.multiple_of(r0, 16), 16), :] = hi
            dst[pl.ds(pl.multiple_of(128 + r0, 16), 16), :] = (v - hi.astype(F32)).astype(BF16)

    def ry(u, hf):
        dev2 = (dev_y3, dev_y1)[hf]
        wait(f"r1{u}.{hf}", rb1.at[u, hf])
        base = 4 * f1[hf]
        o = 2 * (1 - f2[hf])
        pbuf[u, hf, pl.ds(base + o, 2)] = pbuf[u, hf, pl.ds(base + o, 2)] + rb1[u, hf, pl.ds(o, 2)]
        send(f"r2{u}.{hf}", pbuf.at[u, hf, pl.ds(base + o, 2)], rb2.at[u, hf], dev2)
        o = 2 * f2[hf]
        vbuf[u, hf] = pbuf[u, hf, pl.ds(base + o, 2)] + rb1[u, hf, pl.ds(o, 2)]

    def xhi(u, s):
        for i in range(2):
            wait(f"a{u}.{i}", ab.at[u, i])
        vbuf[u, xh] = vbuf[u, xh] + ab[u]
        for hf in range(2):
            wait(f"r2{u}.{hf}", rb2.at[u, hf])
            vbuf[u, hf] = vbuf[u, hf] + rb2[u, hf]
        send(f"xh{u}", vbuf.at[u], xb.at[u], dev_xh)

    def ay1(u, s):
        wait(f"xh{u}", xb.at[u])
        for hf, dev in ((0, dev_y3), (1, dev_y1)):
            slot = c1all.at[u, hf, pl.ds(2 * q[hf], 2)]
            c1all[u, hf, pl.ds(2 * q[hf], 2)] = vbuf[u, hf] + xb[u, hf]
            send(f"g1{u}.{hf}", slot, slot, dev)
        for i in range(2):
            move(f"cs{u}.{i}", sem(f"c{u}.0") + hpart, c1all.at[u, xh, 2 * md + i], ci.at[u, hpart], dev_zz[i])

    def rel(u, s):
        move(f"as{u}", sem(f"am{u}"), a_ref.at[u], ai.at[u], dev_mid)

    def rel2(u, s):
        wait(f"am{u}", ai.at[u])
        for h in range(2):
            src = ai.at[u, :, pl.ds(h * KR, KR)]
            move(f"at{u}.{h}", sem(f"a{u}.0") + hpart, src, ab.at[u, hpart], dev_zz[h])

    def crel(u, s):
        for h in range(2):
            wait(f"c{u}.{h}", ci.at[u, h])
        move(f"ct{u}", sem(f"ch{u}"), ci.at[u], ch.at[u], dev_home)

    def ay2(u, hf):
        dev2 = (dev_y1, dev_y3)[hf]
        o = 4 * f1[hf] + 2 * (1 - f2[hf])
        wait(f"g1{u}.{hf}", c1all.at[u, hf, pl.ds(o, 2)])
        slot = c1all.at[u, hf, pl.ds(4 * f1[hf], 4)]
        send(f"g2{u}.{hf}", slot, slot, dev2)

    def mmt_part(u, c0, n):
        r = lax.dot_general(cs_ref[...], hhi[:, pl.ds(c0, n)], NN, preferred_element_type=F32)
        r2 = lax.dot_general(cs_ref[:128], hlo[:, pl.ds(c0, n)], NN, preferred_element_type=F32)
        qbuf[u, :, :, :, pl.ds(c0, n)] = (r[:128] + r[128:] + r2).reshape(2, 8, 8, n)

    def mmt(u, s):
        if s == 0:
            for hf in range(2):
                wait(f"g2{u}.{hf}", c1all.at[u, hf, pl.ds(4 * (1 - f1[hf]), 4)])
            for half in range(2):
                split_half(c1all, u, half, cs_ref, KR)

            @pl.loop(0, 4)
            def _(j):
                mmt_part(u, pl.multiple_of(j * 256, 256), 256)

            for o in (4, -3, 3, -2, 2, -1, 1, 0):
                send(f"y{u}.{o}", qbuf.at[u, xo, zi(o), :, LO], rx1.at[u, zi(o)], dev_x)
            return

        @pl.loop(4, 7)
        def _(j):
            mmt_part(u, pl.multiple_of(j * 256, 256), 256)

        send(f"ha{u}.1", qbuf.at[u, xo, zi(3), :, HI], rpa.at[u, 0], dev_a)
        send(f"hb{u}.1", qbuf.at[u, xo, zi(-4), :, HI], rpb.at[u, 0], dev_b)

    def take_x(u, o):
        wait(f"y{u}.{o}", rx1.at[u, zi(o)])
        qbuf[u, x, zi(o), :, LO] = qbuf[u, x, zi(o), :, LO] + rx1[u, zi(o)]

    def add(u, o, buf, j):
        qbuf[u, x, zi(o)] = qbuf[u, x, zi(o)] + buf[u, j]

    def addh(u, o, buf, j):
        qbuf[u, xo, zi(o), :, HI] = qbuf[u, xo, zi(o), :, HI] + buf[u, j]

    def ra(u, s):
        o = 5 - s
        take_x(u, o)
        if s > 1:
            wait(f"za{u}.{s - 1}", rza.at[u, s - 2])
            add(u, o, rza, s - 2)
        send(f"za{u}.{s}", qbuf.at[u, x, zi(o)], rza.at[u, s - 1], dev_a)

    def rb(u, s):
        o = -(4 - s)
        take_x(u, o)
        if s > 1:
            wait(f"zb{u}.{s - 1}", rzb.at[u, s - 2])
            add(u, o, rzb, s - 2)
        send(f"zb{u}.{s}", qbuf.at[u, x, zi(o)], rzb.at[u, s - 1], dev_b)

    def rpa_(u, s):
        wait(f"ha{u}.{s}", rpa.at[u, s - 1])
        o = 3 - s
        addh(u, o, rpa, s - 1)
        if s < 3:
            send(f"ha{u}.{s + 1}", qbuf.at[u, xo, zi(o), :, HI], rpa.at[u, s], dev_a)

    def rpb_(u, s):
        wait(f"hb{u}.{s}", rpb.at[u, s - 1])
        o = -(4 - s)
        addh(u, o, rpb, s - 1)
        if s < 4:
            send(f"hb{u}.{s + 1}", qbuf.at[u, xo, zi(o), :, HI], rpb.at[u, s], dev_b)

    def rpf(u, s):
        rpa_(u, 3)
        rpb_(u, 4)
        send(f"xf{u}", qbuf.at[u, xo, z, :, HI], rxf.at[u], dev_x)

    def fin(u, s):
        take_x(u, 0)
        wait(f"zb{u}.3", rzb.at[u, 2])
        wait(f"za{u}.4", rza.at[u, 3])
        wait(f"xf{u}", rxf.at[u])
        v = qbuf[u, x, z] + rza[u, 3] + rzb[u, 2]
        g1_out[u, :, LO] = v[:, :KR]
        g1_out[u, :, HI] = v[:, KR:] + rxf[u]
        wait(f"ch{u}", ch.at[u])
        for h in range(2):
            c1_out[u, :, pl.ds(h * KR, KR)] = ch[u, h]

    for u in range(U):
        for i in range(2):
            sem(f"a{u}.{i}")
        for i in range(2):
            sem(f"c{u}.{i}")

    stages = dict(
        ag0=ag0, ga=ga, gb=gb, gx=gx, gpa=gpa, gpb=gpb, mm=mm, ry=ry, xhi=xhi, ay1=ay1, ay2=ay2,
        mmt=mmt, ra=ra, rb=rb, rpa=rpa_, rpb=rpb_, rpf=rpf, fin=fin, rel=rel, rel2=rel2, crel=crel,
    )
    pl.semaphore_wait(barrier, expected)
    ag0(0, 0)
    loads[4].wait()
    send("h", h_ref, hbuf.at[k], dev_core)
    split_rows(k)
    for name, u, s in ORDER:
        stages[name](u, s)
    for c in sends:
        c.wait_send()
    for c, same in moves:

        @pl.when(jnp.logical_not(same))
        def _():
            c.wait_send()

    assert len(names) <= NSEM, len(names)


NSEM = 320


def run_kernel(h, *arrays):
    v = pltpu.VMEM
    scratch = [
        v((U, 8, KC), F32), v((U, 8, KC), F32), v((U, 8, KC), F32), v((U, 8, KC), jnp.int32),
        v((U, 8, KC), F32), v((U, 8, KC), F32),
        v((2, 448, KC), F32), v((KR, KC), BF16), v((KR, KC), BF16), v((256, KC), BF16),
        v((U, 2, 8, 8, KC), F32),
        v((U, 2, 8, 8, KR), F32),
        v((U, 2, 4, 8, KR), F32), v((U, 2, 2, 8, KR), F32),
        v((U, 2, 2, 8, KR), F32), v((U, 2, 2, 8, KR), F32),
        v((U, 2, 8, 8, KR), F32), v((256, KR), BF16),
        v((U, 2, 8, 8, KC), F32),
        v((U, 8, 8, KR), F32),
        v((U, 4, 8, KC), F32), v((U, 3, 8, KC), F32),
        v((U, 3, 8, KR), F32), v((U, 4, 8, KR), F32),
        v((U, 8, KR), F32),
        v((U, 2, 8, KR), F32), v((U, 2, 8, KR), F32),
        v((U, 8, KC), F32), v((U, 2, 8, KR), F32),
        pltpu.SemaphoreType.DMA((NSEM,)), pltpu.SemaphoreType.DMA((NSEM,)),
        pltpu.SemaphoreType.DMA((5,)),
    ]
    return pl.pallas_call(
        kernel,
        out_shape=[jax.ShapeDtypeStruct((U, 8, KC), F32)] * 2,
        in_specs=[pl.BlockSpec(memory_space=pl.ANY)] * 5,
        out_specs=[pl.BlockSpec(memory_space=pltpu.VMEM)] * 2,
        scratch_shapes=scratch,
        compiler_params=pltpu.CompilerParams(
            collective_id=0, has_side_effects=True, vmem_limit_bytes=56 * 1024 * 1024
        ),
    )(h, *(t.reshape(U, 8, KC) for t in arrays))


def per_device(hessian, dense_weight, start_iterate, start_multiplier, keep_mask):
    weight, iterate0, multiplier0 = dense_weight.T, start_iterate.T, start_multiplier.T
    keeping = keep_mask.T.astype(F32)
    c1, g1 = run_kernel(hessian, weight, iterate0, multiplier0, keep_mask.T)
    iterate1 = c1.reshape(32, KC) + weight
    projected1 = keeping * (iterate1 + multiplier0)
    multiplier1 = multiplier0 + iterate1 - projected1
    iterate2 = iterate1 - STEP * (g1.reshape(32, KC) + (iterate1 - projected1 + multiplier1))
    projected2 = keeping * (iterate2 + multiplier1)
    multiplier2 = multiplier1 + iterate2 - projected2
    return iterate2.T, projected2.T, multiplier2.T


def solution(mesh):
    return jax.shard_map(
        per_device,
        mesh=mesh,
        in_specs=(P("row", "col"),) + (P("col", "row"),) * 4,
        out_specs=(P("col", "row"),) * 3,
        check_vma=False,
    )
```

```python
import math

import jax
import jax.numpy as jnp
from jax import lax
from jax.experimental import pallas as pl
from jax.experimental.pallas import tpu as pltpu
from jax.sharding import PartitionSpec as P

MESH = pl.DeviceIdType.MESH
STEP = 0.25
U = 4
KC = 1792
KR = 896
F32 = jnp.float32
BF16 = jnp.bfloat16


ORDER = (
    ("ag0", 1, 0), ("ag0", 2, 0), ("ag0", 3, 0), ("gx", 0, 0), ("rel", 0, 0), ("ga", 0, 1), ("gb", 0, 1),
    ("gx", 1, 0), ("rel", 1, 0), ("gb", 1, 1), ("ga", 1, 1), ("gx", 2, 0), ("rel", 2, 0), ("ga", 2, 1),
    ("gb", 2, 1), ("gx", 3, 0), ("rel", 3, 0), ("ga", 3, 1), ("gb", 3, 1), ("gpa", 0, 1), ("gpb", 0, 1),
    ("gb", 0, 2), ("ga", 0, 2), ("gpb", 1, 1), ("gpa", 1, 1), ("gb", 1, 2), ("ga", 1, 2), ("gpa", 2, 1),
    ("gpb", 2, 1), ("ga", 2, 2), ("gb", 2, 2), ("gpb", 3, 1), ("gpa", 3, 1), ("ga", 3, 2), ("gb", 3, 2),
    ("gpb", 0, 2), ("gpa", 0, 2), ("ga", 0, 3), ("gb", 0, 3), ("gpa", 1, 2), ("gpb", 1, 2), ("gb", 1, 3),
    ("ga", 1, 3), ("gpb", 2, 2), ("gpa", 2, 2), ("gb", 2, 3), ("ga", 2, 3), ("gpb", 3, 2), ("gpa", 3, 2),
    ("ga", 3, 3), ("gb", 3, 3), ("rel2", 0, 0), ("rel2", 1, 0), ("gpb", 0, 3), ("rel2", 2, 0), ("rel2", 3, 0),
    ("gpb", 1, 3), ("ga", 0, 4), ("gpb", 2, 3), ("gpb", 3, 3), ("ga", 1, 4), ("mm", 0, 0), ("ga", 2, 4),
    ("ga", 3, 4), ("mm", 0, 1), ("mm", 1, 0), ("mm", 1, 1), ("ry", 0, 0), ("ry", 0, 2), ("ry", 0, 1),
    ("ry", 0, 3), ("mm", 2, 0), ("ry", 1, 0), ("ry", 1, 2), ("mm", 2, 1), ("xhi", 0, 0), ("ry", 1, 3),
    ("xhi", 0, 1), ("ry", 1, 1), ("mm", 3, 0), ("xhi", 1, 0), ("ry", 2, 2), ("ry", 2, 0), ("mm", 3, 1),
    ("xhi", 1, 1), ("ay1", 0, 0), ("ry", 2, 1), ("ry", 2, 3), ("ay1", 0, 1), ("crel0", 0, 0), ("ry", 3, 0),
    ("ry", 3, 2), ("xhi", 2, 0), ("ay1", 1, 0), ("ry", 3, 1), ("ry", 3, 3), ("ay2", 0, 0), ("ay2", 0, 2),
    ("ay1", 1, 1), ("xhi", 2, 1), ("crel0", 1, 0), ("ay2", 0, 1), ("ay2", 0, 3), ("xhi", 3, 0), ("ay2", 1, 0),
    ("ay2", 1, 2), ("ay1", 2, 0), ("xhi", 3, 1), ("crel", 0, 0), ("ay2", 1, 1), ("ay2", 1, 3), ("ay1", 2, 1),
    ("crel0", 2, 0), ("mmt", 0, 0), ("ay2", 2, 0), ("ay2", 2, 2), ("ay1", 3, 0), ("ay1", 3, 1),
    ("crel", 1, 0), ("crel0", 3, 0), ("mmt", 0, 1), ("ra", 0, 1), ("ay2", 2, 1), ("ay2", 2, 3), ("mmt", 1, 0),
    ("rb", 0, 1), ("ay2", 3, 2), ("ay2", 3, 0), ("crel", 2, 0), ("ay2", 3, 3), ("rpa", 0, 1), ("rpb", 0, 1),
    ("ay2", 3, 1), ("mmt", 1, 1), ("ra", 0, 2), ("ra", 1, 1), ("crel", 3, 0), ("mmt", 2, 0), ("rb", 0, 2),
    ("rpa", 0, 2), ("rpb", 0, 2), ("rb", 1, 1), ("rpb", 1, 1), ("rpa", 1, 1), ("mmt", 2, 1), ("ra", 0, 3),
    ("mmt", 3, 0), ("rb", 0, 3), ("rpb", 0, 3), ("ra", 1, 2), ("rpa", 1, 2), ("ra", 2, 1), ("rb", 2, 1),
    ("rpa", 2, 1), ("rb", 1, 2), ("mmt", 3, 1), ("ra", 0, 4), ("rpb", 1, 2), ("rpb", 2, 1), ("ra", 3, 1),
    ("rb", 3, 1), ("ra", 1, 3), ("rpf", 0, 0), ("rb", 2, 2), ("ra", 2, 2), ("rb", 1, 3), ("rpa", 2, 2),
    ("rpa", 3, 1), ("rpb", 3, 1), ("rpb", 1, 3), ("fin", 0, 0), ("rpb", 2, 2), ("ra", 3, 2), ("rb", 3, 2),
    ("ra", 1, 4), ("rb", 2, 3), ("ra", 2, 3), ("rpb", 3, 2), ("rpa", 3, 2), ("rpf", 1, 0), ("rpb", 2, 3),
    ("ra", 3, 3), ("rb", 3, 3), ("fin", 1, 0), ("ra", 2, 4), ("rpb", 3, 3), ("rpf", 2, 0), ("ra", 3, 4),
    ("rpf", 3, 0), ("fin", 2, 0), ("fin", 3, 0),
)


def kernel(
    h_ref, w_ref, i_ref, m_ref, k_ref, c1_out, g1_out,
    wv, iv, mv, kv, c0_ref, a_ref,
    hbuf, hhi, hlo, xs_ref, xall, pbuf, rb1, rb2, vbuf, xb, c1all, cs_ref, qbuf,
    rx1, rza, rzb, rpa, rpb, rxf, ab, ch, ai, ci, tally, ss, rs, hs, bulk,
):
    row = lax.axis_index("row")
    col = lax.axis_index("col")
    k = row % 2
    z = (row // 2) % 8
    x = row // 16
    y = col // 2
    xh = col % 2
    d = 1 - 2 * k
    xo = 1 - x

    def zi(off):
        return (z + d * off + 16) % 8

    def dev_z(off):
        return (x * 16 + zi(off) * 2 + k, col)

    dev_a, dev_b = dev_z(1), dev_z(-1)
    dev_x = (xo * 16 + z * 2 + k, col)
    dev_core = (x * 16 + z * 2 + (1 - k), col)
    y1 = y + 1 - 2 * (y % 2)
    y3 = 3 - y
    dev_y1 = (row, y1 * 2 + xh)
    dev_y3 = (row, y3 * 2 + xh)
    dev_xh = (row, y * 2 + (1 - xh))

    b0, b1 = y % 2, y // 2
    bx = (b0 + b1) % 2
    m0, m1 = (z // 2) % 2, z // 4
    f1 = ((bx + m1) % 2, (b1 + m1) % 2)
    f2 = ((1 - b1 + m0) % 2, (1 - b0 + m0) % 2)
    q = (2 * f1[0] + f2[0], 2 * f1[1] + f2[1])
    q0 = (2 * bx + 1 - b1, 2 * b1 + 1 - b0)

    cblk = y * 2 + xh
    e0, e1 = (z // 2 + cblk) % 2, (z // 4 + (cblk % 4) // 2) % 2
    ya_b1 = 1 - e0
    ya_b0 = (e1 + ya_b1) % 2
    y_if0 = 2 * ya_b1 + ya_b0
    y_if1 = 2 * e1 + (1 - e0)
    yd = (1 - x) * y_if0 + x * y_if1
    qx = (1 - xh) * q0[0] + xh * q0[1]
    md = 2 * ((qx // 2 + z // 4) % 2) + (qx + z // 2) % 2
    dev_mid = ((y // 2) * 16 + z * 2 + k, yd * 2 + x)
    dev_home = (xh * 16 + z * 2 + k, 4 * x + md)
    dev_zz = [(x * 16 + (2 * md + h) * 2 + k, col) for h in range(2)]

    def here(dev):
        return jnp.logical_and(dev[0] == row, dev[1] == col)

    hpart = z % 2

    barrier = pltpu.get_barrier_semaphore()
    peers = [dev_a, dev_b, dev_x, dev_core, dev_y1, dev_y3, dev_xh]
    for p in peers:
        pl.semaphore_signal(barrier, inc=1, device_id=p, device_id_type=MESH)
    expected = len(peers)
    for p in [dev_mid, dev_home] + dev_zz:
        same = here(p)
        expected = expected + 1 - same.astype(jnp.int32)

        @pl.when(jnp.logical_not(same))
        def _():
            pl.semaphore_signal(barrier, inc=1, device_id=p, device_id_type=MESH)

    loads = [
        pltpu.make_async_copy(src, dst, hs.at[n])
        for n, (src, dst) in enumerate(((w_ref, wv), (i_ref, iv), (m_ref, mv), (k_ref, kv), (h_ref, hbuf.at[k])))
    ]
    for c in loads:
        c.start()
    loads[0].wait()
    loads[1].wait()
    for u in range(U):
        c0_ref[u] = iv[u] - wv[u]
    loads[2].wait()
    loads[3].wait()
    for u in range(U):
        v0, m0 = iv[u], mv[u]
        p0 = kv[u].astype(F32) * (v0 + m0)
        a_ref[u] = c0_ref[u] - STEP * (v0 - p0 + m0)
        xall[u, x, z] = c0_ref[u]

    names = {}
    sent = {}
    moves = []

    def sem(name):
        return names.setdefault(name, len(names))

    def send(name, src, dst, dev):
        i = sem(name)
        u = int(name.split(".")[0][-1]) if name != "h" else U
        sent[u] = sent.get(u, 0) + math.prod(src.shape)
        pltpu.make_async_remote_copy(
            src_ref=src, dst_ref=dst, send_sem=bulk.at[u], recv_sem=rs.at[i],
            device_id=dev, device_id_type=MESH,
        ).start()

    def move(name, recv, src, dst, dev):
        i = sem(name)
        same = here(dev)
        c = pltpu.make_async_remote_copy(
            src_ref=src, dst_ref=dst, send_sem=ss.at[i], recv_sem=rs.at[recv],
            device_id=dev, device_id_type=MESH,
        )

        @pl.when(jnp.logical_not(same))
        def _():
            c.start()

        @pl.when(same)
        def _():
            pltpu.make_async_copy(src, dst, rs.at[recv]).start()

        moves.append((c, same))

    def wait(name, slot):
        i = sem(name)
        pltpu.make_async_remote_copy(
            src_ref=slot, dst_ref=slot, send_sem=ss.at[i], recv_sem=rs.at[i],
            device_id=dev_x, device_id_type=MESH,
        ).wait_recv()

    LO = pl.ds(0, KR)
    HI = pl.ds(KR, KR)
    COLS = (pl.ds(0, 512), pl.ds(512, 384))

    def split_rows(part):
        @pl.loop(0, 28)
        def _(i):
            r0 = pl.multiple_of(i * 16, 16)
            v = hbuf[part, pl.ds(r0, 16), :]
            hi = v.astype(BF16)
            o0 = pl.multiple_of(part * 448 + i * 16, 16)
            hhi[pl.ds(o0, 16), :] = hi
            hlo[pl.ds(o0, 16), :] = (v - hi.astype(F32)).astype(BF16)

    def full(u, o):
        return xall.at[u, x, zi(o)]

    def par(u, o):
        return xall.at[u, xo, zi(o), :, HI]

    def low(u, o):
        return xall.at[u, x, zi(o), :, LO]

    def ag0(u, s):
        send(f"fa{u}.1", c0_ref.at[u], full(u, 0), dev_a)
        send(f"fb{u}.1", c0_ref.at[u], full(u, 0), dev_b)
        send(f"x{u}", c0_ref.at[u], full(u, 0), dev_x)

    def ga(u, s):
        wait(f"fa{u}.{s}", full(u, -s))
        if s < 4:
            send(f"fa{u}.{s + 1}", full(u, -s), full(u, -s), dev_a)
        send(f"xa{u}.{s}", low(u, -s), low(u, -s), dev_x)

    def gb(u, s):
        wait(f"fb{u}.{s}", full(u, s))
        if s < 3:
            send(f"fb{u}.{s + 1}", full(u, s), full(u, s), dev_b)
        send(f"xb{u}.{s}", low(u, s), low(u, s), dev_x)

    def gx(u, s):
        wait(f"x{u}", xall.at[u, xo, z])
        send(f"pa{u}.1", par(u, 0), par(u, 0), dev_a)
        send(f"pb{u}.1", par(u, 0), par(u, 0), dev_b)

    def gpa(u, s):
        wait(f"pa{u}.{s}", par(u, -s))
        send(f"pa{u}.{s + 1}", par(u, -s), par(u, -s), dev_a)

    def gpb(u, s):
        wait(f"pb{u}.{s}", par(u, s))
        send(f"pb{u}.{s + 1}", par(u, s), par(u, s), dev_b)

    def wait_gather(u):
        wait(f"pa{u}.3", par(u, -3))
        wait(f"pb{u}.4", par(u, 4))
        olow = lambda o: xall.at[u, xo, zi(o), :, LO]
        for j in range(1, 5):
            wait(f"xa{u}.{j}", olow(-j))
        for j in range(1, 4):
            wait(f"xb{u}.{j}", olow(j))

    NT = (((1,), (1,)), ((), ()))
    NN = (((1,), (0,)), ((), ()))

    def mm_part(u, c0, n):
        r = lax.dot_general(xs_ref[...], hhi[pl.ds(c0, n), :], NT, preferred_element_type=F32)
        r2 = lax.dot_general(xs_ref[:128], hlo[pl.ds(c0, n), :], NT, preferred_element_type=F32)
        v = (r[:128] + r[128:] + r2) * (-STEP)
        pbuf[u, :, :, :, pl.ds(c0, n)] = v.reshape(2, 8, 8, n)

    def mm(u, s):
        if s == 0:
            wait_gather(u)
            if u == 0:
                wait("h", hbuf.at[1 - k])
                split_rows(1 - k)
            for half in range(2):
                split_half(xall, u, half, xs_ref, KC)

            @pl.loop(0, 2)
            def _(j):
                mm_part(u, pl.multiple_of(j * 256, 256), 256)
        else:
            mm_part(u, 512, 256)
            mm_part(u, 768, 128)
        for hf, dev in ((0, dev_y1), (1, dev_y3)):
            src = pbuf.at[u, hf, pl.ds(4 * (1 - f1[hf]), 4), :, COLS[s]]
            send(f"r1{u}.{hf}{s}", src, rb1.at[u, hf, :, :, COLS[s]], dev)

    def split_half(src, u, half, dst, width):
        @pl.loop(0, 4)
        def _(i):
            v = src[u, half, pl.ds(i * 2, 2)].reshape(16, width)
            hi = v.astype(BF16)
            r0 = half * 64 + i * 16
            dst[pl.ds(pl.multiple_of(r0, 16), 16), :] = hi
            dst[pl.ds(pl.multiple_of(128 + r0, 16), 16), :] = (v - hi.astype(F32)).astype(BF16)

    def ry(u, s):
        hf, cc = s // 2, COLS[s % 2]
        dev2 = (dev_y3, dev_y1)[hf]
        wait(f"r1{u}.{hf}{s % 2}", rb1.at[u, hf, :, :, cc])
        base = 4 * f1[hf]
        o = 2 * (1 - f2[hf])
        pair = pl.ds(base + o, 2)
        pbuf[u, hf, pair, :, cc] = pbuf[u, hf, pair, :, cc] + rb1[u, hf, pl.ds(o, 2), :, cc]
        send(f"r2{u}.{hf}{s % 2}", pbuf.at[u, hf, pair, :, cc], rb2.at[u, hf, :, :, cc], dev2)
        o = 2 * f2[hf]
        vbuf[u, hf, :, :, cc] = pbuf[u, hf, pl.ds(base + o, 2), :, cc] + rb1[u, hf, pl.ds(o, 2), :, cc]

    def xhi(u, s):
        cc = COLS[s]
        if s == 0:
            for i in range(2):
                wait(f"a{u}.{i}", ab.at[u, i])
        vbuf[u, xh, :, :, cc] = vbuf[u, xh, :, :, cc] + ab[u, :, :, cc]
        for hf in range(2):
            wait(f"r2{u}.{hf}{s}", rb2.at[u, hf, :, :, cc])
            vbuf[u, hf, :, :, cc] = vbuf[u, hf, :, :, cc] + rb2[u, hf, :, :, cc]
        send(f"xh{u}.{s}", vbuf.at[u, :, :, :, cc], xb.at[u, :, :, :, cc], dev_xh)

    def ay1(u, s):
        cc = COLS[s]
        wait(f"xh{u}.{s}", xb.at[u, :, :, :, cc])
        for hf, dev in ((0, dev_y3), (1, dev_y1)):
            slot = c1all.at[u, hf, pl.ds(2 * q[hf], 2), :, cc]
            c1all[u, hf, pl.ds(2 * q[hf], 2), :, cc] = vbuf[u, hf, :, :, cc] + xb[u, hf, :, :, cc]
            send(f"g1{u}.{hf}{s}", slot, slot, dev)

    def crel0(u, s):
        for i in range(2):
            move(f"cs{u}.{i}", sem(f"c{u}.0") + hpart, c1all.at[u, xh, 2 * md + i], ci.at[u, hpart], dev_zz[i])

    def rel(u, s):
        move(f"as{u}", sem(f"am{u}"), a_ref.at[u], ai.at[u], dev_mid)

    def rel2(u, s):
        wait(f"am{u}", ai.at[u])
        for h in range(2):
            src = ai.at[u, :, pl.ds(h * KR, KR)]
            move(f"at{u}.{h}", sem(f"a{u}.0") + hpart, src, ab.at[u, hpart], dev_zz[h])

    def crel(u, s):
        for h in range(2):
            wait(f"c{u}.{h}", ci.at[u, h])
        move(f"ct{u}", sem(f"ch{u}"), ci.at[u], ch.at[u], dev_home)

    def ay2(u, s):
        hf, cc = s // 2, COLS[s % 2]
        dev2 = (dev_y1, dev_y3)[hf]
        o = 4 * f1[hf] + 2 * (1 - f2[hf])
        wait(f"g1{u}.{hf}{s % 2}", c1all.at[u, hf, pl.ds(o, 2), :, cc])
        slot = c1all.at[u, hf, pl.ds(4 * f1[hf], 4), :, cc]
        send(f"g2{u}.{hf}{s % 2}", slot, slot, dev2)

    def mmt_part(u, c0, n):
        r = lax.dot_general(cs_ref[...], hhi[:, pl.ds(c0, n)], NN, preferred_element_type=F32)
        r2 = lax.dot_general(cs_ref[:128], hlo[:, pl.ds(c0, n)], NN, preferred_element_type=F32)
        qbuf[u, :, :, :, pl.ds(c0, n)] = (r[:128] + r[128:] + r2).reshape(2, 8, 8, n)

    def mmt(u, s):
        if s == 0:
            for hf in range(2):
                for c in range(2):
                    wait(f"g2{u}.{hf}{c}", c1all.at[u, hf, pl.ds(4 * (1 - f1[hf]), 4), :, COLS[c]])
            for half in range(2):
                split_half(c1all, u, half, cs_ref, KR)

            @pl.loop(0, 4)
            def _(j):
                mmt_part(u, pl.multiple_of(j * 256, 256), 256)

            for o in (4, -3, 3, -2, 2, -1, 1, 0):
                send(f"y{u}.{o}", qbuf.at[u, xo, zi(o), :, LO], rx1.at[u, zi(o)], dev_x)
            return

        @pl.loop(4, 7)
        def _(j):
            mmt_part(u, pl.multiple_of(j * 256, 256), 256)

        send(f"ha{u}.1", qbuf.at[u, xo, zi(3), :, HI], rpa.at[u, 0], dev_a)
        send(f"hb{u}.1", qbuf.at[u, xo, zi(-4), :, HI], rpb.at[u, 0], dev_b)

    def take_x(u, o):
        wait(f"y{u}.{o}", rx1.at[u, zi(o)])
        qbuf[u, x, zi(o), :, LO] = qbuf[u, x, zi(o), :, LO] + rx1[u, zi(o)]

    def add(u, o, buf, j):
        qbuf[u, x, zi(o)] = qbuf[u, x, zi(o)] + buf[u, j]

    def addh(u, o, buf, j):
        qbuf[u, xo, zi(o), :, HI] = qbuf[u, xo, zi(o), :, HI] + buf[u, j]

    def ra(u, s):
        o = 5 - s
        take_x(u, o)
        if s > 1:
            wait(f"za{u}.{s - 1}", rza.at[u, s - 2])
            add(u, o, rza, s - 2)
        send(f"za{u}.{s}", qbuf.at[u, x, zi(o)], rza.at[u, s - 1], dev_a)

    def rb(u, s):
        o = -(4 - s)
        take_x(u, o)
        if s > 1:
            wait(f"zb{u}.{s - 1}", rzb.at[u, s - 2])
            add(u, o, rzb, s - 2)
        send(f"zb{u}.{s}", qbuf.at[u, x, zi(o)], rzb.at[u, s - 1], dev_b)

    def rpa_(u, s):
        wait(f"ha{u}.{s}", rpa.at[u, s - 1])
        o = 3 - s
        addh(u, o, rpa, s - 1)
        if s < 3:
            send(f"ha{u}.{s + 1}", qbuf.at[u, xo, zi(o), :, HI], rpa.at[u, s], dev_a)

    def rpb_(u, s):
        wait(f"hb{u}.{s}", rpb.at[u, s - 1])
        o = -(4 - s)
        addh(u, o, rpb, s - 1)
        if s < 4:
            send(f"hb{u}.{s + 1}", qbuf.at[u, xo, zi(o), :, HI], rpb.at[u, s], dev_b)

    def rpf(u, s):
        rpa_(u, 3)
        rpb_(u, 4)
        send(f"xf{u}", qbuf.at[u, xo, z, :, HI], rxf.at[u], dev_x)

    def fin(u, s):
        take_x(u, 0)
        wait(f"zb{u}.3", rzb.at[u, 2])
        wait(f"za{u}.4", rza.at[u, 3])
        wait(f"xf{u}", rxf.at[u])
        v = qbuf[u, x, z] + rza[u, 3] + rzb[u, 2]
        g1_out[u, :, LO] = v[:, :KR]
        g1_out[u, :, HI] = v[:, KR:] + rxf[u]
        wait(f"ch{u}", ch.at[u])
        for h in range(2):
            c1_out[u, :, pl.ds(h * KR, KR)] = ch[u, h]

    for u in range(U):
        for i in range(2):
            sem(f"a{u}.{i}")
        for i in range(2):
            sem(f"c{u}.{i}")

    stages = dict(
        ag0=ag0, ga=ga, gb=gb, gx=gx, gpa=gpa, gpb=gpb, mm=mm, ry=ry, xhi=xhi, ay1=ay1, ay2=ay2,
        mmt=mmt, ra=ra, rb=rb, rpa=rpa_, rpb=rpb_, rpf=rpf, fin=fin, rel=rel, rel2=rel2, crel0=crel0, crel=crel,
    )
    pl.semaphore_wait(barrier, expected)
    ag0(0, 0)
    loads[4].wait()
    send("h", h_ref, hbuf.at[k], dev_core)
    split_rows(k)
    for name, u, s in ORDER:
        stages[name](u, s)
    for u in range(U):
        assert sent[u] == math.prod(tally.shape), sent
        pltpu.make_async_copy(tally, tally, bulk.at[u]).wait()
    pltpu.make_async_copy(h_ref, hbuf.at[k], bulk.at[U]).wait()
    for c, same in moves:

        @pl.when(jnp.logical_not(same))
        def _():
            c.wait_send()

    assert len(names) <= NSEM, len(names)


NSEM = 320


def run_kernel(h, *arrays):
    v = pltpu.VMEM
    scratch = [
        v((U, 8, KC), F32), v((U, 8, KC), F32), v((U, 8, KC), F32), v((U, 8, KC), jnp.int32),
        v((U, 8, KC), F32), v((U, 8, KC), F32),
        v((2, 448, KC), F32), v((KR, KC), BF16), v((KR, KC), BF16), v((256, KC), BF16),
        v((U, 2, 8, 8, KC), F32),
        v((U, 2, 8, 8, KR), F32),
        v((U, 2, 4, 8, KR), F32), v((U, 2, 2, 8, KR), F32),
        v((U, 2, 2, 8, KR), F32), v((U, 2, 2, 8, KR), F32),
        v((U, 2, 8, 8, KR), F32), v((256, KR), BF16),
        v((U, 2, 8, 8, KC), F32),
        v((U, 8, 8, KR), F32),
        v((U, 4, 8, KC), F32), v((U, 3, 8, KC), F32),
        v((U, 3, 8, KR), F32), v((U, 4, 8, KR), F32),
        v((U, 8, KR), F32),
        v((U, 2, 8, KR), F32), v((U, 2, 8, KR), F32),
        v((U, 8, KC), F32), v((U, 2, 8, KR), F32),
        v((44, 8, KC), F32),
        pltpu.SemaphoreType.DMA((NSEM,)), pltpu.SemaphoreType.DMA((NSEM,)),
        pltpu.SemaphoreType.DMA((5,)), pltpu.SemaphoreType.DMA((U + 1,)),
    ]
    return pl.pallas_call(
        kernel,
        out_shape=[jax.ShapeDtypeStruct((U, 8, KC), F32)] * 2,
        in_specs=[pl.BlockSpec(memory_space=pl.ANY)] * 5,
        out_specs=[pl.BlockSpec(memory_space=pltpu.VMEM)] * 2,
        scratch_shapes=scratch,
        compiler_params=pltpu.CompilerParams(
            collective_id=0, has_side_effects=True, vmem_limit_bytes=56 * 1024 * 1024
        ),
    )(h, *(t.reshape(U, 8, KC) for t in arrays))


def per_device(hessian, dense_weight, start_iterate, start_multiplier, keep_mask):
    weight, iterate0, multiplier0 = dense_weight.T, start_iterate.T, start_multiplier.T
    keeping = keep_mask.T.astype(F32)
    c1, g1 = run_kernel(hessian, weight, iterate0, multiplier0, keep_mask.T)
    iterate1 = c1.reshape(32, KC) + weight
    projected1 = keeping * (iterate1 + multiplier0)
    multiplier1 = multiplier0 + iterate1 - projected1
    iterate2 = iterate1 - STEP * (g1.reshape(32, KC) + (iterate1 - projected1 + multiplier1))
    projected2 = keeping * (iterate2 + multiplier1)
    multiplier2 = multiplier1 + iterate2 - projected2
    return iterate2.T, projected2.T, multiplier2.T


def solution(mesh):
    return jax.shard_map(
        per_device,
        mesh=mesh,
        in_specs=(P("row", "col"),) + (P("col", "row"),) * 4,
        out_specs=(P("col", "row"),) * 3,
        check_vma=False,
    )
```

```python
import math

import jax
import jax.numpy as jnp
from jax import lax
from jax.experimental import pallas as pl
from jax.experimental.pallas import tpu as pltpu
from jax.sharding import PartitionSpec as P

MESH = pl.DeviceIdType.MESH
STEP = 0.25
U = 4
KC = 1792
KR = 896
F32 = jnp.float32
BF16 = jnp.bfloat16


ORDER = (
    ("ag0", 1, 0), ("ag0", 2, 0), ("gx", 0, 0), ("rel", 0, 0), ("ga", 0, 1), ("gb", 0, 1), ("gx", 1, 0),
    ("rel", 1, 0), ("ga", 1, 1), ("gb", 1, 1), ("gx", 2, 0), ("rel", 2, 0), ("ga", 2, 1), ("gb", 2, 1),
    ("gpa", 0, 1), ("gpb", 0, 1), ("ga", 0, 2), ("gb", 0, 2), ("gpb", 1, 1), ("gpa", 1, 1), ("ga", 1, 2),
    ("gb", 1, 2), ("gpb", 2, 1), ("gpa", 2, 1), ("ag0", 3, 0), ("ga", 2, 2), ("gb", 2, 2), ("gpb", 0, 2),
    ("gpa", 0, 2), ("ga", 0, 3), ("gb", 0, 3), ("gx", 3, 0), ("gpb", 1, 2), ("gpa", 1, 2), ("rel", 3, 0),
    ("ga", 1, 3), ("gb", 1, 3), ("gpa", 2, 2), ("gpb", 2, 2), ("ga", 3, 1), ("gb", 3, 1), ("hs", 0, 0),
    ("ga", 2, 3), ("gb", 2, 3), ("gpb", 0, 3), ("gpb", 3, 1), ("ga", 0, 4), ("gpb", 1, 3), ("gpb", 2, 3),
    ("gpa", 3, 1), ("gb", 3, 2), ("ga", 1, 4), ("mm", 0, 0), ("ga", 3, 2), ("gpb", 3, 2), ("rel2", 0, 0),
    ("rel2", 3, 0), ("mm", 0, 1), ("ga", 2, 4), ("gb", 3, 3), ("gpa", 3, 2), ("mm", 1, 0), ("ry", 0, 0),
    ("ry", 0, 2), ("ga", 3, 3), ("gpb", 3, 3), ("mm", 2, 0), ("ry", 0, 3), ("ry", 0, 1), ("mm", 1, 1),
    ("ry", 1, 2), ("ry", 1, 0), ("rel2", 1, 0), ("ga", 3, 4), ("xhi", 0, 0), ("rel2", 2, 0), ("mm", 2, 1),
    ("ry", 2, 0), ("ry", 2, 2), ("xhi", 0, 1), ("mm", 3, 0), ("ry", 1, 1), ("ry", 1, 3), ("mm", 3, 1),
    ("ay1", 0, 0), ("ry", 2, 3), ("ry", 2, 1), ("xhi", 1, 0), ("ay1", 0, 1), ("crel0", 0, 0), ("xhi", 2, 0),
    ("ry", 3, 0), ("ry", 3, 2), ("xhi", 1, 1), ("ry", 3, 1), ("ry", 3, 3), ("ay2", 0, 0), ("ay2", 0, 2),
    ("xhi", 2, 1), ("ay1", 1, 0), ("ay2", 0, 1), ("ay2", 0, 3), ("xhi", 3, 0), ("ay1", 2, 0), ("xhi", 3, 1),
    ("crel", 0, 0), ("ay1", 1, 1), ("crel0", 1, 0), ("ay2", 1, 0), ("ay2", 1, 2), ("ay1", 2, 1),
    ("crel0", 2, 0), ("mmt", 0, 0), ("ay2", 1, 1), ("ay2", 1, 3), ("ay1", 3, 1), ("ay2", 2, 0), ("ay1", 3, 0),
    ("ay2", 2, 2), ("mmt", 0, 1), ("ay2", 2, 1), ("ay2", 2, 3), ("crel0", 3, 0), ("ra", 0, 1), ("crel", 1, 0),
    ("rb", 0, 1), ("mmt", 1, 0), ("rpa", 0, 1), ("rpb", 0, 1), ("ay2", 3, 3), ("ay2", 3, 1), ("ay2", 3, 0),
    ("mmt", 1, 1), ("ra", 0, 2), ("rb", 0, 2), ("ay2", 3, 2), ("mmt", 2, 0), ("rpa", 0, 2), ("rpb", 0, 2),
    ("ra", 1, 1), ("rb", 1, 1), ("mmt", 2, 1), ("rpb", 1, 1), ("rpa", 1, 1), ("rb", 0, 3), ("ra", 0, 3),
    ("mmt", 3, 0), ("rpb", 0, 3), ("ra", 1, 2), ("rb", 1, 2), ("ra", 2, 1), ("rb", 2, 1), ("rpa", 2, 1),
    ("rpb", 2, 1), ("mmt", 3, 1), ("rpa", 1, 2), ("ra", 0, 4), ("rpb", 1, 2), ("crel", 2, 0), ("crel", 3, 0),
    ("rpf", 0, 0), ("ra", 3, 1), ("ra", 1, 3), ("rb", 3, 1), ("rb", 1, 3), ("ra", 2, 2), ("rb", 2, 2),
    ("rpa", 2, 2), ("rpb", 2, 2), ("rpa", 3, 1), ("rpb", 3, 1), ("rpb", 1, 3), ("fin", 0, 0), ("rb", 3, 2),
    ("ra", 3, 2), ("ra", 1, 4), ("rb", 2, 3), ("rpb", 2, 3), ("ra", 2, 3), ("rpb", 3, 2), ("rpf", 1, 0),
    ("rpa", 3, 2), ("rb", 3, 3), ("ra", 3, 3), ("fin", 1, 0), ("rpf", 2, 0), ("rpb", 3, 3), ("ra", 2, 4),
    ("ra", 3, 4), ("rpf", 3, 0), ("fin", 2, 0), ("fin", 3, 0),
)


def kernel(
    h_ref, w_ref, i_ref, m_ref, k_ref, c1_out, g1_out,
    wv, iv, mv, kv, c0_ref, a_ref,
    hbuf, hhi, hlo, xs_ref, xall, pbuf, rb1, rb2, vbuf, xb, c1all, cs_ref, qbuf,
    rx1, rza, rzb, rpa, rpb, rxf, ab, ch, ai, ci, tally, ss, rs, hs, bulk,
):
    row = lax.axis_index("row")
    col = lax.axis_index("col")
    k = row % 2
    z = (row // 2) % 8
    x = row // 16
    y = col // 2
    xh = col % 2
    d = 1 - 2 * k
    xo = 1 - x

    def zi(off):
        return (z + d * off + 16) % 8

    def dev_z(off):
        return (x * 16 + zi(off) * 2 + k, col)

    dev_a, dev_b = dev_z(1), dev_z(-1)
    dev_x = (xo * 16 + z * 2 + k, col)
    dev_core = (x * 16 + z * 2 + (1 - k), col)
    y1 = y + 1 - 2 * (y % 2)
    y3 = 3 - y
    dev_y1 = (row, y1 * 2 + xh)
    dev_y3 = (row, y3 * 2 + xh)
    dev_xh = (row, y * 2 + (1 - xh))

    b0, b1 = y % 2, y // 2
    bx = (b0 + b1) % 2
    m0, m1 = (z // 2) % 2, z // 4
    f1 = ((bx + m1) % 2, (b1 + m1) % 2)
    f2 = ((1 - b1 + m0) % 2, (1 - b0 + m0) % 2)
    q = (2 * f1[0] + f2[0], 2 * f1[1] + f2[1])
    q0 = (2 * bx + 1 - b1, 2 * b1 + 1 - b0)

    cblk = y * 2 + xh
    e0, e1 = (z // 2 + cblk) % 2, (z // 4 + (cblk % 4) // 2) % 2
    ya_b1 = 1 - e0
    ya_b0 = (e1 + ya_b1) % 2
    y_if0 = 2 * ya_b1 + ya_b0
    y_if1 = 2 * e1 + (1 - e0)
    yd = (1 - x) * y_if0 + x * y_if1
    qx = (1 - xh) * q0[0] + xh * q0[1]
    md = 2 * ((qx // 2 + z // 4) % 2) + (qx + z // 2) % 2
    dev_mid = ((y // 2) * 16 + z * 2 + k, yd * 2 + x)
    dev_home = (xh * 16 + z * 2 + k, 4 * x + md)
    dev_zz = [(x * 16 + (2 * md + h) * 2 + k, col) for h in range(2)]

    def here(dev):
        return jnp.logical_and(dev[0] == row, dev[1] == col)

    hpart = z % 2

    barrier = pltpu.get_barrier_semaphore()
    peers = [dev_a, dev_b, dev_x, dev_core, dev_y1, dev_y3, dev_xh]
    for p in peers:
        pl.semaphore_signal(barrier, inc=1, device_id=p, device_id_type=MESH)
    expected = len(peers)
    for p in [dev_mid, dev_home] + dev_zz:
        same = here(p)
        expected = expected + 1 - same.astype(jnp.int32)

        @pl.when(jnp.logical_not(same))
        def _():
            pl.semaphore_signal(barrier, inc=1, device_id=p, device_id_type=MESH)

    loads = [
        pltpu.make_async_copy(src, dst, hs.at[n])
        for n, (src, dst) in enumerate(((w_ref, wv), (i_ref, iv), (m_ref, mv), (k_ref, kv), (h_ref, hbuf.at[k])))
    ]
    for c in loads:
        c.start()
    loads[0].wait()
    loads[1].wait()
    for u in range(U):
        c0_ref[u] = iv[u] - wv[u]
    loads[2].wait()
    loads[3].wait()
    for u in range(U):
        v0, m0 = iv[u], mv[u]
        p0 = kv[u].astype(F32) * (v0 + m0)
        a_ref[u] = c0_ref[u] - STEP * (v0 - p0 + m0)
        xall[u, x, z] = c0_ref[u]

    names = {}
    sent = {}
    moves = []

    def sem(name):
        return names.setdefault(name, len(names))

    def send(name, src, dst, dev):
        i = sem(name)
        u = int(name.split(".")[0][-1]) if name != "h" else U
        sent[u] = sent.get(u, 0) + math.prod(src.shape)
        pltpu.make_async_remote_copy(
            src_ref=src, dst_ref=dst, send_sem=bulk.at[u], recv_sem=rs.at[i],
            device_id=dev, device_id_type=MESH,
        ).start()

    def move(name, recv, src, dst, dev):
        i = sem(name)
        same = here(dev)
        c = pltpu.make_async_remote_copy(
            src_ref=src, dst_ref=dst, send_sem=ss.at[i], recv_sem=rs.at[recv],
            device_id=dev, device_id_type=MESH,
        )

        @pl.when(jnp.logical_not(same))
        def _():
            c.start()

        @pl.when(same)
        def _():
            pltpu.make_async_copy(src, dst, rs.at[recv]).start()

        moves.append((c, same))

    def wait(name, slot):
        i = sem(name)
        pltpu.make_async_remote_copy(
            src_ref=slot, dst_ref=slot, send_sem=ss.at[i], recv_sem=rs.at[i],
            device_id=dev_x, device_id_type=MESH,
        ).wait_recv()

    LO = pl.ds(0, KR)
    HI = pl.ds(KR, KR)
    COLS = (pl.ds(0, 512), pl.ds(512, 384))

    def split_rows(part):
        @pl.loop(0, 28)
        def _(i):
            r0 = pl.multiple_of(i * 16, 16)
            v = hbuf[part, pl.ds(r0, 16), :]
            hi = v.astype(BF16)
            o0 = pl.multiple_of(part * 448 + i * 16, 16)
            hhi[pl.ds(o0, 16), :] = hi
            hlo[pl.ds(o0, 16), :] = (v - hi.astype(F32)).astype(BF16)

    def full(u, o):
        return xall.at[u, x, zi(o)]

    def par(u, o):
        return xall.at[u, xo, zi(o), :, HI]

    def low(u, o):
        return xall.at[u, x, zi(o), :, LO]

    def ag0(u, s):
        send(f"fa{u}.1", c0_ref.at[u], full(u, 0), dev_a)
        send(f"fb{u}.1", c0_ref.at[u], full(u, 0), dev_b)
        send(f"x{u}", c0_ref.at[u], full(u, 0), dev_x)

    def ga(u, s):
        wait(f"fa{u}.{s}", full(u, -s))
        if s < 4:
            send(f"fa{u}.{s + 1}", full(u, -s), full(u, -s), dev_a)
        send(f"xa{u}.{s}", low(u, -s), low(u, -s), dev_x)

    def gb(u, s):
        wait(f"fb{u}.{s}", full(u, s))
        if s < 3:
            send(f"fb{u}.{s + 1}", full(u, s), full(u, s), dev_b)
        send(f"xb{u}.{s}", low(u, s), low(u, s), dev_x)

    def gx(u, s):
        wait(f"x{u}", xall.at[u, xo, z])
        send(f"pa{u}.1", par(u, 0), par(u, 0), dev_a)
        send(f"pb{u}.1", par(u, 0), par(u, 0), dev_b)

    def gpa(u, s):
        wait(f"pa{u}.{s}", par(u, -s))
        send(f"pa{u}.{s + 1}", par(u, -s), par(u, -s), dev_a)

    def gpb(u, s):
        wait(f"pb{u}.{s}", par(u, s))
        send(f"pb{u}.{s + 1}", par(u, s), par(u, s), dev_b)

    def wait_gather(u):
        wait(f"pa{u}.3", par(u, -3))
        wait(f"pb{u}.4", par(u, 4))
        olow = lambda o: xall.at[u, xo, zi(o), :, LO]
        for j in range(1, 5):
            wait(f"xa{u}.{j}", olow(-j))
        for j in range(1, 4):
            wait(f"xb{u}.{j}", olow(j))

    NT = (((1,), (1,)), ((), ()))
    NN = (((1,), (0,)), ((), ()))

    def mm_part(u, c0, n):
        r = lax.dot_general(xs_ref[u], hhi[pl.ds(c0, n), :], NT, preferred_element_type=F32)
        r2 = lax.dot_general(xs_ref[u, :128], hlo[pl.ds(c0, n), :], NT, preferred_element_type=F32)
        v = (r[:128] + r[128:] + r2) * (-STEP)
        pbuf[u, :, :, :, pl.ds(c0, n)] = v.reshape(2, 8, 8, n)

    def mm(u, s):
        if s == 0:
            wait_gather(u)
            for half in range(2):
                split_half(xall, u, half, xs_ref.at[u], KC)

            @pl.loop(0, 2)
            def _(j):
                mm_part(u, pl.multiple_of(j * 256, 256), 256)
        else:
            mm_part(u, 512, 256)
            mm_part(u, 768, 128)
        for hf, dev in ((0, dev_y1), (1, dev_y3)):
            src = pbuf.at[u, hf, pl.ds(4 * (1 - f1[hf]), 4), :, COLS[s]]
            send(f"r1{u}.{hf}{s}", src, rb1.at[u, hf, :, :, COLS[s]], dev)

    def hs_(u, s):
        wait("h", hbuf.at[1 - k])
        split_rows(1 - k)

    def split_half(src, u, half, dst, width):
        @pl.loop(0, 4)
        def _(i):
            v = src[u, half, pl.ds(i * 2, 2)].reshape(16, width)
            hi = v.astype(BF16)
            r0 = half * 64 + i * 16
            dst[pl.ds(pl.multiple_of(r0, 16), 16), :] = hi
            dst[pl.ds(pl.multiple_of(128 + r0, 16), 16), :] = (v - hi.astype(F32)).astype(BF16)

    def ry(u, s):
        hf, cc = s // 2, COLS[s % 2]
        dev2 = (dev_y3, dev_y1)[hf]
        wait(f"r1{u}.{hf}{s % 2}", rb1.at[u, hf, :, :, cc])
        base = 4 * f1[hf]
        o = 2 * (1 - f2[hf])
        pair = pl.ds(base + o, 2)
        pbuf[u, hf, pair, :, cc] = pbuf[u, hf, pair, :, cc] + rb1[u, hf, pl.ds(o, 2), :, cc]
        send(f"r2{u}.{hf}{s % 2}", pbuf.at[u, hf, pair, :, cc], rb2.at[u, hf, :, :, cc], dev2)
        o = 2 * f2[hf]
        vbuf[u, hf, :, :, cc] = pbuf[u, hf, pl.ds(base + o, 2), :, cc] + rb1[u, hf, pl.ds(o, 2), :, cc]

    def xhi(u, s):
        cc = COLS[s]
        if s == 0:
            for i in range(2):
                wait(f"a{u}.{i}", ab.at[u, i])
        vbuf[u, xh, :, :, cc] = vbuf[u, xh, :, :, cc] + ab[u, :, :, cc]
        for hf in range(2):
            wait(f"r2{u}.{hf}{s}", rb2.at[u, hf, :, :, cc])
            vbuf[u, hf, :, :, cc] = vbuf[u, hf, :, :, cc] + rb2[u, hf, :, :, cc]
        send(f"xh{u}.{s}", vbuf.at[u, :, :, :, cc], xb.at[u, :, :, :, cc], dev_xh)

    def ay1(u, s):
        cc = COLS[s]
        wait(f"xh{u}.{s}", xb.at[u, :, :, :, cc])
        for hf, dev in ((0, dev_y3), (1, dev_y1)):
            slot = c1all.at[u, hf, pl.ds(2 * q[hf], 2), :, cc]
            c1all[u, hf, pl.ds(2 * q[hf], 2), :, cc] = vbuf[u, hf, :, :, cc] + xb[u, hf, :, :, cc]
            send(f"g1{u}.{hf}{s}", slot, slot, dev)

    def crel0(u, s):
        for i in range(2):
            move(f"cs{u}.{i}", sem(f"c{u}.0") + hpart, c1all.at[u, xh, 2 * md + i], ci.at[u, hpart], dev_zz[i])

    def rel(u, s):
        move(f"as{u}", sem(f"am{u}"), a_ref.at[u], ai.at[u], dev_mid)

    def rel2(u, s):
        wait(f"am{u}", ai.at[u])
        for h in range(2):
            src = ai.at[u, :, pl.ds(h * KR, KR)]
            move(f"at{u}.{h}", sem(f"a{u}.0") + hpart, src, ab.at[u, hpart], dev_zz[h])

    def crel(u, s):
        for h in range(2):
            wait(f"c{u}.{h}", ci.at[u, h])
        move(f"ct{u}", sem(f"ch{u}"), ci.at[u], ch.at[u], dev_home)

    def ay2(u, s):
        hf, cc = s // 2, COLS[s % 2]
        dev2 = (dev_y1, dev_y3)[hf]
        o = 4 * f1[hf] + 2 * (1 - f2[hf])
        wait(f"g1{u}.{hf}{s % 2}", c1all.at[u, hf, pl.ds(o, 2), :, cc])
        slot = c1all.at[u, hf, pl.ds(4 * f1[hf], 4), :, cc]
        send(f"g2{u}.{hf}{s % 2}", slot, slot, dev2)

    def mmt_part(u, c0, n):
        r = lax.dot_general(cs_ref[u], hhi[:, pl.ds(c0, n)], NN, preferred_element_type=F32)
        r2 = lax.dot_general(cs_ref[u, :128], hlo[:, pl.ds(c0, n)], NN, preferred_element_type=F32)
        qbuf[u, :, :, :, pl.ds(c0, n)] = (r[:128] + r[128:] + r2).reshape(2, 8, 8, n)

    def mmt(u, s):
        if s == 0:
            for hf in range(2):
                for c in range(2):
                    wait(f"g2{u}.{hf}{c}", c1all.at[u, hf, pl.ds(4 * (1 - f1[hf]), 4), :, COLS[c]])
            for half in range(2):
                split_half(c1all, u, half, cs_ref.at[u], KR)

            @pl.loop(0, 4)
            def _(j):
                mmt_part(u, pl.multiple_of(j * 256, 256), 256)

            for o in (4, -3, 3, -2, 2, -1, 1, 0):
                send(f"y{u}.{o}", qbuf.at[u, xo, zi(o), :, LO], rx1.at[u, zi(o)], dev_x)
            return

        @pl.loop(4, 7)
        def _(j):
            mmt_part(u, pl.multiple_of(j * 256, 256), 256)

        send(f"ha{u}.1", qbuf.at[u, xo, zi(3), :, HI], rpa.at[u, 0], dev_a)
        send(f"hb{u}.1", qbuf.at[u, xo, zi(-4), :, HI], rpb.at[u, 0], dev_b)

    def take_x(u, o):
        wait(f"y{u}.{o}", rx1.at[u, zi(o)])
        qbuf[u, x, zi(o), :, LO] = qbuf[u, x, zi(o), :, LO] + rx1[u, zi(o)]

    def add(u, o, buf, j):
        qbuf[u, x, zi(o)] = qbuf[u, x, zi(o)] + buf[u, j]

    def addh(u, o, buf, j):
        qbuf[u, xo, zi(o), :, HI] = qbuf[u, xo, zi(o), :, HI] + buf[u, j]

    def ra(u, s):
        o = 5 - s
        take_x(u, o)
        if s > 1:
            wait(f"za{u}.{s - 1}", rza.at[u, s - 2])
            add(u, o, rza, s - 2)
        send(f"za{u}.{s}", qbuf.at[u, x, zi(o)], rza.at[u, s - 1], dev_a)

    def rb(u, s):
        o = -(4 - s)
        take_x(u, o)
        if s > 1:
            wait(f"zb{u}.{s - 1}", rzb.at[u, s - 2])
            add(u, o, rzb, s - 2)
        send(f"zb{u}.{s}", qbuf.at[u, x, zi(o)], rzb.at[u, s - 1], dev_b)

    def rpa_(u, s):
        wait(f"ha{u}.{s}", rpa.at[u, s - 1])
        o = 3 - s
        addh(u, o, rpa, s - 1)
        if s < 3:
            send(f"ha{u}.{s + 1}", qbuf.at[u, xo, zi(o), :, HI], rpa.at[u, s], dev_a)

    def rpb_(u, s):
        wait(f"hb{u}.{s}", rpb.at[u, s - 1])
        o = -(4 - s)
        addh(u, o, rpb, s - 1)
        if s < 4:
            send(f"hb{u}.{s + 1}", qbuf.at[u, xo, zi(o), :, HI], rpb.at[u, s], dev_b)

    def rpf(u, s):
        rpa_(u, 3)
        rpb_(u, 4)
        send(f"xf{u}", qbuf.at[u, xo, z, :, HI], rxf.at[u], dev_x)

    def fin(u, s):
        take_x(u, 0)
        wait(f"zb{u}.3", rzb.at[u, 2])
        wait(f"za{u}.4", rza.at[u, 3])
        wait(f"xf{u}", rxf.at[u])
        v = qbuf[u, x, z] + rza[u, 3] + rzb[u, 2]
        g1_out[u, :, LO] = v[:, :KR]
        g1_out[u, :, HI] = v[:, KR:] + rxf[u]
        wait(f"ch{u}", ch.at[u])
        for h in range(2):
            c1_out[u, :, pl.ds(h * KR, KR)] = ch[u, h]

    for u in range(U):
        for i in range(2):
            sem(f"a{u}.{i}")
        for i in range(2):
            sem(f"c{u}.{i}")

    stages = dict(
        ag0=ag0, ga=ga, gb=gb, gx=gx, gpa=gpa, gpb=gpb, mm=mm, ry=ry, xhi=xhi, ay1=ay1, ay2=ay2,
        mmt=mmt, ra=ra, rb=rb, rpa=rpa_, rpb=rpb_, rpf=rpf, fin=fin, hs=hs_, rel=rel, rel2=rel2, crel0=crel0, crel=crel,
    )
    pl.semaphore_wait(barrier, expected)
    ag0(0, 0)
    loads[4].wait()
    send("h", h_ref, hbuf.at[k], dev_core)
    split_rows(k)
    for name, u, s in ORDER:
        stages[name](u, s)
    for u in range(U):
        assert sent[u] == math.prod(tally.shape), sent
        pltpu.make_async_copy(tally, tally, bulk.at[u]).wait()
    pltpu.make_async_copy(h_ref, hbuf.at[k], bulk.at[U]).wait()
    for c, same in moves:

        @pl.when(jnp.logical_not(same))
        def _():
            c.wait_send()

    assert len(names) <= NSEM, len(names)


NSEM = 320


def run_kernel(h, *arrays):
    v = pltpu.VMEM
    scratch = [
        v((U, 8, KC), F32), v((U, 8, KC), F32), v((U, 8, KC), F32), v((U, 8, KC), jnp.int32),
        v((U, 8, KC), F32), v((U, 8, KC), F32),
        v((2, 448, KC), F32), v((KR, KC), BF16), v((KR, KC), BF16), v((U, 256, KC), BF16),
        v((U, 2, 8, 8, KC), F32),
        v((U, 2, 8, 8, KR), F32),
        v((U, 2, 4, 8, KR), F32), v((U, 2, 2, 8, KR), F32),
        v((U, 2, 2, 8, KR), F32), v((U, 2, 2, 8, KR), F32),
        v((U, 2, 8, 8, KR), F32), v((U, 256, KR), BF16),
        v((U, 2, 8, 8, KC), F32),
        v((U, 8, 8, KR), F32),
        v((U, 4, 8, KC), F32), v((U, 3, 8, KC), F32),
        v((U, 3, 8, KR), F32), v((U, 4, 8, KR), F32),
        v((U, 8, KR), F32),
        v((U, 2, 8, KR), F32), v((U, 2, 8, KR), F32),
        v((U, 8, KC), F32), v((U, 2, 8, KR), F32),
        v((44, 8, KC), F32),
        pltpu.SemaphoreType.DMA((NSEM,)), pltpu.SemaphoreType.DMA((NSEM,)),
        pltpu.SemaphoreType.DMA((5,)), pltpu.SemaphoreType.DMA((U + 1,)),
    ]
    return pl.pallas_call(
        kernel,
        out_shape=[jax.ShapeDtypeStruct((U, 8, KC), F32)] * 2,
        in_specs=[pl.BlockSpec(memory_space=pl.ANY)] * 5,
        out_specs=[pl.BlockSpec(memory_space=pltpu.VMEM)] * 2,
        scratch_shapes=scratch,
        compiler_params=pltpu.CompilerParams(
            collective_id=0, has_side_effects=True, vmem_limit_bytes=56 * 1024 * 1024
        ),
    )(h, *(t.reshape(U, 8, KC) for t in arrays))


def per_device(hessian, dense_weight, start_iterate, start_multiplier, keep_mask):
    weight, iterate0, multiplier0 = dense_weight.T, start_iterate.T, start_multiplier.T
    keeping = keep_mask.T.astype(F32)
    c1, g1 = run_kernel(hessian, weight, iterate0, multiplier0, keep_mask.T)
    iterate1 = c1.reshape(32, KC) + weight
    projected1 = keeping * (iterate1 + multiplier0)
    multiplier1 = multiplier0 + iterate1 - projected1
    iterate2 = iterate1 - STEP * (g1.reshape(32, KC) + (iterate1 - projected1 + multiplier1))
    projected2 = keeping * (iterate2 + multiplier1)
    multiplier2 = multiplier1 + iterate2 - projected2
    return iterate2.T, projected2.T, multiplier2.T


def solution(mesh):
    return jax.shard_map(
        per_device,
        mesh=mesh,
        in_specs=(P("row", "col"),) + (P("col", "row"),) * 4,
        out_specs=(P("col", "row"),) * 3,
        check_vma=False,
    )
```

```python
import math

import jax
import jax.numpy as jnp
from jax import lax
from jax.experimental import pallas as pl
from jax.experimental.pallas import tpu as pltpu
from jax.sharding import PartitionSpec as P

MESH = pl.DeviceIdType.MESH
STEP = 0.25
U = 4
KC = 1792
KR = 896
F32 = jnp.float32
BF16 = jnp.bfloat16


ORDER = (
    ("ag0", 1, 0), ("ag0", 2, 0), ("gx", 0, 0), ("rel", 0, 0), ("ga", 0, 1), ("gb", 0, 1), ("gx", 1, 0),
    ("rel", 1, 0), ("ga", 1, 1), ("gb", 1, 1), ("gx", 2, 0), ("rel", 2, 0), ("ga", 2, 1), ("gb", 2, 1),
    ("gpa", 0, 1), ("gpb", 0, 1), ("ga", 0, 2), ("gb", 0, 2), ("gpb", 1, 1), ("gpa", 1, 1), ("ga", 1, 2),
    ("gb", 1, 2), ("gpb", 2, 1), ("gpa", 2, 1), ("ag0", 3, 0), ("ga", 2, 2), ("gb", 2, 2), ("gpb", 0, 2),
    ("gpa", 0, 2), ("ga", 0, 3), ("gb", 0, 3), ("gx", 3, 0), ("gpb", 1, 2), ("gpa", 1, 2), ("rel", 3, 0),
    ("ga", 1, 3), ("gb", 1, 3), ("gpa", 2, 2), ("gpb", 2, 2), ("ga", 3, 1), ("gb", 3, 1), ("hs", 0, 0),
    ("ga", 2, 3), ("gb", 2, 3), ("gpb", 0, 3), ("gpb", 3, 1), ("ga", 0, 4), ("gpb", 1, 3), ("gpb", 2, 3),
    ("gpa", 3, 1), ("gb", 3, 2), ("ga", 1, 4), ("mm", 0, 0), ("ga", 3, 2), ("gpb", 3, 2), ("rel2", 0, 0),
    ("rel2", 3, 0), ("mm", 0, 1), ("ga", 2, 4), ("gb", 3, 3), ("gpa", 3, 2), ("mm", 1, 0), ("ry", 0, 0),
    ("ry", 0, 2), ("ga", 3, 3), ("gpb", 3, 3), ("mm", 2, 0), ("ry", 0, 3), ("ry", 0, 1), ("mm", 1, 1),
    ("ry", 1, 2), ("ry", 1, 0), ("rel2", 1, 0), ("ga", 3, 4), ("xhi", 0, 0), ("rel2", 2, 0), ("mm", 2, 1),
    ("ry", 2, 0), ("ry", 2, 2), ("xhi", 0, 1), ("mm", 3, 0), ("ry", 1, 1), ("ry", 1, 3), ("mm", 3, 1),
    ("ay1", 0, 0), ("ry", 2, 3), ("ry", 2, 1), ("xhi", 1, 0), ("ay1", 0, 1), ("crel0", 0, 0), ("xhi", 2, 0),
    ("ry", 3, 0), ("ry", 3, 2), ("xhi", 1, 1), ("ry", 3, 1), ("ry", 3, 3), ("ay2", 0, 0), ("ay2", 0, 2),
    ("xhi", 2, 1), ("ay1", 1, 0), ("ay2", 0, 1), ("ay2", 0, 3), ("xhi", 3, 0), ("ay1", 2, 0), ("xhi", 3, 1),
    ("crel", 0, 0), ("ay1", 1, 1), ("crel0", 1, 0), ("ay2", 1, 0), ("ay2", 1, 2), ("ay1", 2, 1),
    ("crel0", 2, 0), ("mmt", 0, 0), ("ay2", 1, 1), ("ay2", 1, 3), ("ay1", 3, 1), ("ay2", 2, 0), ("ay1", 3, 0),
    ("ay2", 2, 2), ("mmt", 0, 1), ("ay2", 2, 1), ("ay2", 2, 3), ("crel0", 3, 0), ("ra", 0, 1), ("crel", 1, 0),
    ("rb", 0, 1), ("mmt", 1, 0), ("rpa", 0, 1), ("rpb", 0, 1), ("ay2", 3, 3), ("ay2", 3, 1), ("ay2", 3, 0),
    ("mmt", 1, 1), ("ra", 0, 2), ("rb", 0, 2), ("ay2", 3, 2), ("mmt", 2, 0), ("rpa", 0, 2), ("rpb", 0, 2),
    ("ra", 1, 1), ("rb", 1, 1), ("mmt", 2, 1), ("rpb", 1, 1), ("rpa", 1, 1), ("rb", 0, 3), ("ra", 0, 3),
    ("mmt", 3, 0), ("rpb", 0, 3), ("ra", 1, 2), ("rb", 1, 2), ("ra", 2, 1), ("rb", 2, 1), ("rpa", 2, 1),
    ("rpb", 2, 1), ("mmt", 3, 1), ("rpa", 1, 2), ("ra", 0, 4), ("rpb", 1, 2), ("crel", 2, 0), ("crel", 3, 0),
    ("rpf", 0, 0), ("ra", 3, 1), ("ra", 1, 3), ("rb", 3, 1), ("rb", 1, 3), ("ra", 2, 2), ("rb", 2, 2),
    ("rpa", 2, 2), ("rpb", 2, 2), ("rpa", 3, 1), ("rpb", 3, 1), ("rpb", 1, 3), ("fin", 0, 0), ("rb", 3, 2),
    ("ra", 3, 2), ("ra", 1, 4), ("rb", 2, 3), ("rpb", 2, 3), ("ra", 2, 3), ("rpb", 3, 2), ("rpf", 1, 0),
    ("rpa", 3, 2), ("rb", 3, 3), ("ra", 3, 3), ("fin", 1, 0), ("rpf", 2, 0), ("rpb", 3, 3), ("ra", 2, 4),
    ("ra", 3, 4), ("rpf", 3, 0), ("fin", 2, 0), ("fin", 3, 0),
)


def kernel(
    h_ref, w_ref, i_ref, m_ref, k_ref, c1_out, g1_out,
    wv, iv, mv, kv, c0_ref, a_ref,
    hbuf, hhi, hlo, xs_ref, xall, pbuf, rb1, rb2, vbuf, xb, c1all, cs_ref, qbuf,
    rx1, rza, rzb, rpa, rpb, rxf, ab, ch, ai, ci, tally, ss, rs, hs, bulk,
):
    row = lax.axis_index("row")
    col = lax.axis_index("col")
    k = row % 2
    z = (row // 2) % 8
    x = row // 16
    y = col // 2
    xh = col % 2
    d = 1 - 2 * k
    xo = 1 - x

    def zi(off):
        return (z + d * off + 16) % 8

    def dev_z(off):
        return (x * 16 + zi(off) * 2 + k, col)

    dev_a, dev_b = dev_z(1), dev_z(-1)
    dev_x = (xo * 16 + z * 2 + k, col)
    dev_core = (x * 16 + z * 2 + (1 - k), col)
    y1 = y + 1 - 2 * (y % 2)
    y3 = 3 - y
    dev_y1 = (row, y1 * 2 + xh)
    dev_y3 = (row, y3 * 2 + xh)
    dev_xh = (row, y * 2 + (1 - xh))

    b0, b1 = y % 2, y // 2
    bx = (b0 + b1) % 2
    m0, m1 = (z // 2) % 2, z // 4
    f1 = ((bx + m1) % 2, (b1 + m1) % 2)
    f2 = ((1 - b1 + m0) % 2, (1 - b0 + m0) % 2)
    q = (2 * f1[0] + f2[0], 2 * f1[1] + f2[1])
    q0 = (2 * bx + 1 - b1, 2 * b1 + 1 - b0)

    cblk = y * 2 + xh
    e0, e1 = (z // 2 + cblk) % 2, (z // 4 + (cblk % 4) // 2) % 2
    ya_b1 = 1 - e0
    ya_b0 = (e1 + ya_b1) % 2
    y_if0 = 2 * ya_b1 + ya_b0
    y_if1 = 2 * e1 + (1 - e0)
    yd = (1 - x) * y_if0 + x * y_if1
    qx = (1 - xh) * q0[0] + xh * q0[1]
    md = 2 * ((qx // 2 + z // 4) % 2) + (qx + z // 2) % 2
    dev_mid = ((y // 2) * 16 + z * 2 + k, yd * 2 + x)
    dev_home = (xh * 16 + z * 2 + k, 4 * x + md)
    dev_zz = [(x * 16 + (2 * md + h) * 2 + k, col) for h in range(2)]

    def here(dev):
        return jnp.logical_and(dev[0] == row, dev[1] == col)

    hpart = z % 2

    barrier = pltpu.get_barrier_semaphore()
    peers = [dev_a, dev_b, dev_x, dev_core, dev_y1, dev_y3, dev_xh]
    for p in peers:
        pl.semaphore_signal(barrier, inc=1, device_id=p, device_id_type=MESH)
    expected = len(peers)
    for p in [dev_mid, dev_home] + dev_zz:
        same = here(p)
        expected = expected + 1 - same.astype(jnp.int32)

        @pl.when(jnp.logical_not(same))
        def _():
            pl.semaphore_signal(barrier, inc=1, device_id=p, device_id_type=MESH)

    loads = [
        pltpu.make_async_copy(src, dst, hs.at[n])
        for n, (src, dst) in enumerate(((w_ref, wv), (i_ref, iv), (m_ref, mv), (k_ref, kv), (h_ref, hbuf.at[k])))
    ]
    for c in loads:
        c.start()
    loads[0].wait()
    loads[1].wait()
    for u in range(U):
        c0_ref[u] = iv[u] - wv[u]
    loads[2].wait()
    loads[3].wait()
    for u in range(U):
        v0, m0 = iv[u], mv[u]
        p0 = kv[u].astype(F32) * (v0 + m0)
        a_ref[u] = c0_ref[u] - STEP * (v0 - p0 + m0)
        xall[u, x, z] = c0_ref[u]

    names = {}
    sent = {}
    moves = []

    def sem(name):
        return names.setdefault(name, len(names))

    def send(name, src, dst, dev):
        i = sem(name)
        u = int(name.split(".")[0][-1]) if name != "h" else U
        sent[u] = sent.get(u, 0) + math.prod(src.shape)
        pltpu.make_async_remote_copy(
            src_ref=src, dst_ref=dst, send_sem=bulk.at[u], recv_sem=rs.at[i],
            device_id=dev, device_id_type=MESH,
        ).start()

    def move(name, recv, src, dst, dev):
        i = sem(name)
        same = here(dev)
        c = pltpu.make_async_remote_copy(
            src_ref=src, dst_ref=dst, send_sem=ss.at[i], recv_sem=rs.at[recv],
            device_id=dev, device_id_type=MESH,
        )

        @pl.when(jnp.logical_not(same))
        def _():
            c.start()

        @pl.when(same)
        def _():
            pltpu.make_async_copy(src, dst, rs.at[recv]).start()

        moves.append((c, same))

    def wait(name, slot):
        i = sem(name)
        pltpu.make_async_remote_copy(
            src_ref=slot, dst_ref=slot, send_sem=ss.at[i], recv_sem=rs.at[i],
            device_id=dev_x, device_id_type=MESH,
        ).wait_recv()

    LO = pl.ds(0, KR)
    HI = pl.ds(KR, KR)
    COLS = (pl.ds(0, 512), pl.ds(512, 384))

    def split_rows(part):
        @pl.loop(0, 28)
        def _(i):
            r0 = pl.multiple_of(i * 16, 16)
            v = hbuf[part, pl.ds(r0, 16), :]
            hi = v.astype(BF16)
            o0 = pl.multiple_of(part * 448 + i * 16, 16)
            hhi[pl.ds(o0, 16), :] = hi
            hlo[pl.ds(o0, 16), :] = (v - hi.astype(F32)).astype(BF16)

    def full(u, o):
        return xall.at[u, x, zi(o)]

    def par(u, o):
        return xall.at[u, xo, zi(o), :, HI]

    def low(u, o):
        return xall.at[u, x, zi(o), :, LO]

    def ag0(u, s):
        send(f"fa{u}.1", c0_ref.at[u], full(u, 0), dev_a)
        send(f"fb{u}.1", c0_ref.at[u], full(u, 0), dev_b)
        send(f"x{u}", c0_ref.at[u], full(u, 0), dev_x)

    def ga(u, s):
        wait(f"fa{u}.{s}", full(u, -s))
        if s < 4:
            send(f"fa{u}.{s + 1}", full(u, -s), full(u, -s), dev_a)
        send(f"xa{u}.{s}", low(u, -s), low(u, -s), dev_x)

    def gb(u, s):
        wait(f"fb{u}.{s}", full(u, s))
        if s < 3:
            send(f"fb{u}.{s + 1}", full(u, s), full(u, s), dev_b)
        send(f"xb{u}.{s}", low(u, s), low(u, s), dev_x)

    def gx(u, s):
        wait(f"x{u}", xall.at[u, xo, z])
        send(f"pa{u}.1", par(u, 0), par(u, 0), dev_a)
        send(f"pb{u}.1", par(u, 0), par(u, 0), dev_b)

    def gpa(u, s):
        wait(f"pa{u}.{s}", par(u, -s))
        send(f"pa{u}.{s + 1}", par(u, -s), par(u, -s), dev_a)

    def gpb(u, s):
        wait(f"pb{u}.{s}", par(u, s))
        send(f"pb{u}.{s + 1}", par(u, s), par(u, s), dev_b)

    def wait_gather(u):
        wait(f"pa{u}.3", par(u, -3))
        wait(f"pb{u}.4", par(u, 4))
        olow = lambda o: xall.at[u, xo, zi(o), :, LO]
        for j in range(1, 5):
            wait(f"xa{u}.{j}", olow(-j))
        for j in range(1, 4):
            wait(f"xb{u}.{j}", olow(j))

    NT = (((1,), (1,)), ((), ()))
    NN = (((1,), (0,)), ((), ()))

    def mm_part(u, c0, n):
        r = lax.dot_general(xs_ref[u], hhi[pl.ds(c0, n), :], NT, preferred_element_type=F32)
        r2 = lax.dot_general(xs_ref[u, :128], hlo[pl.ds(c0, n), :], NT, preferred_element_type=F32)
        v = (r[:128] + r[128:] + r2) * (-STEP)
        pbuf[u, :, :, :, pl.ds(c0, n)] = v.reshape(2, 8, 8, n)

    def mm(u, s):
        if s == 0:
            wait_gather(u)
            for half in range(2):
                split_half(xall, u, half, xs_ref.at[u], KC)

            @pl.loop(0, 2)
            def _(j):
                mm_part(u, pl.multiple_of(j * 256, 256), 256)
        else:
            mm_part(u, 512, 256)
            mm_part(u, 768, 128)
        for hf, dev in ((0, dev_y1), (1, dev_y3)):
            src = pbuf.at[u, hf, pl.ds(4 * (1 - f1[hf]), 4), :, COLS[s]]
            send(f"r1{u}.{hf}{s}", src, rb1.at[u, hf, :, :, COLS[s]], dev)

    def hs_(u, s):
        wait("h", hbuf.at[1 - k])
        split_rows(1 - k)

    def split_half(src, u, half, dst, width):
        @pl.loop(0, 4)
        def _(i):
            v = src[u, half, pl.ds(i * 2, 2)].reshape(16, width)
            hi = v.astype(BF16)
            r0 = half * 64 + i * 16
            dst[pl.ds(pl.multiple_of(r0, 16), 16), :] = hi
            dst[pl.ds(pl.multiple_of(128 + r0, 16), 16), :] = (v - hi.astype(F32)).astype(BF16)

    def ry(u, s):
        hf, cc = s // 2, COLS[s % 2]
        dev2 = (dev_y3, dev_y1)[hf]
        wait(f"r1{u}.{hf}{s % 2}", rb1.at[u, hf, :, :, cc])
        base = 4 * f1[hf]
        o = 2 * (1 - f2[hf])
        pair = pl.ds(base + o, 2)
        pbuf[u, hf, pair, :, cc] = pbuf[u, hf, pair, :, cc] + rb1[u, hf, pl.ds(o, 2), :, cc]
        send(f"r2{u}.{hf}{s % 2}", pbuf.at[u, hf, pair, :, cc], rb2.at[u, hf, :, :, cc], dev2)
        o = 2 * f2[hf]
        vbuf[u, hf, :, :, cc] = pbuf[u, hf, pl.ds(base + o, 2), :, cc] + rb1[u, hf, pl.ds(o, 2), :, cc]

    def xhi(u, s):
        cc = COLS[s]
        if s == 0:
            for i in range(2):
                wait(f"a{u}.{i}", ab.at[u, i])
        vbuf[u, xh, :, :, cc] = vbuf[u, xh, :, :, cc] + ab[u, :, :, cc]
        for hf in range(2):
            wait(f"r2{u}.{hf}{s}", rb2.at[u, hf, :, :, cc])
            vbuf[u, hf, :, :, cc] = vbuf[u, hf, :, :, cc] + rb2[u, hf, :, :, cc]
        send(f"xh{u}.{s}", vbuf.at[u, :, :, :, cc], xb.at[u, :, :, :, cc], dev_xh)

    def ay1(u, s):
        cc = COLS[s]
        wait(f"xh{u}.{s}", xb.at[u, :, :, :, cc])
        for hf, dev in ((0, dev_y3), (1, dev_y1)):
            slot = c1all.at[u, hf, pl.ds(2 * q[hf], 2), :, cc]
            c1all[u, hf, pl.ds(2 * q[hf], 2), :, cc] = vbuf[u, hf, :, :, cc] + xb[u, hf, :, :, cc]
            send(f"g1{u}.{hf}{s}", slot, slot, dev)

    def crel0(u, s):
        for i in range(2):
            move(f"cs{u}.{i}", sem(f"c{u}.0") + hpart, c1all.at[u, xh, 2 * md + i], ci.at[u, hpart], dev_zz[i])

    def rel(u, s):
        move(f"as{u}", sem(f"am{u}"), a_ref.at[u], ai.at[u], dev_mid)

    def rel2(u, s):
        wait(f"am{u}", ai.at[u])
        for h in range(2):
            src = ai.at[u, :, pl.ds(h * KR, KR)]
            move(f"at{u}.{h}", sem(f"a{u}.0") + hpart, src, ab.at[u, hpart], dev_zz[h])

    def crel(u, s):
        for h in range(2):
            wait(f"c{u}.{h}", ci.at[u, h])
        move(f"ct{u}", sem(f"ch{u}"), ci.at[u], ch.at[u], dev_home)

    def ay2(u, s):
        hf, cc = s // 2, COLS[s % 2]
        dev2 = (dev_y1, dev_y3)[hf]
        o = 4 * f1[hf] + 2 * (1 - f2[hf])
        wait(f"g1{u}.{hf}{s % 2}", c1all.at[u, hf, pl.ds(o, 2), :, cc])
        slot = c1all.at[u, hf, pl.ds(4 * f1[hf], 4), :, cc]
        send(f"g2{u}.{hf}{s % 2}", slot, slot, dev2)

    def mmt_part(u, c0, n):
        r = lax.dot_general(cs_ref[u], hhi[:, pl.ds(c0, n)], NN, preferred_element_type=F32)
        r2 = lax.dot_general(cs_ref[u, :128], hlo[:, pl.ds(c0, n)], NN, preferred_element_type=F32)
        qbuf[u, :, :, :, pl.ds(c0, n)] = (r[:128] + r[128:] + r2).reshape(2, 8, 8, n)

    def mmt(u, s):
        if s == 0:
            for hf in range(2):
                for c in range(2):
                    wait(f"g2{u}.{hf}{c}", c1all.at[u, hf, pl.ds(4 * (1 - f1[hf]), 4), :, COLS[c]])
            for half in range(2):
                split_half(c1all, u, half, cs_ref.at[u], KR)

            @pl.loop(0, 4)
            def _(j):
                mmt_part(u, pl.multiple_of(j * 256, 256), 256)

            for o in (4, -3, 3, -2, 2, -1, 1, 0):
                send(f"y{u}.{o}", qbuf.at[u, xo, zi(o), :, LO], rx1.at[u, zi(o)], dev_x)
            return

        @pl.loop(4, 7)
        def _(j):
            mmt_part(u, pl.multiple_of(j * 256, 256), 256)

        send(f"ha{u}.1", qbuf.at[u, xo, zi(3), :, HI], rpa.at[u, 0], dev_a)
        send(f"hb{u}.1", qbuf.at[u, xo, zi(-4), :, HI], rpb.at[u, 0], dev_b)

    def take_x(u, o):
        wait(f"y{u}.{o}", rx1.at[u, zi(o)])
        qbuf[u, x, zi(o), :, LO] = qbuf[u, x, zi(o), :, LO] + rx1[u, zi(o)]

    def add(u, o, buf, j):
        qbuf[u, x, zi(o)] = qbuf[u, x, zi(o)] + buf[u, j]

    def addh(u, o, buf, j):
        qbuf[u, xo, zi(o), :, HI] = qbuf[u, xo, zi(o), :, HI] + buf[u, j]

    def ra(u, s):
        o = 5 - s
        take_x(u, o)
        if s > 1:
            wait(f"za{u}.{s - 1}", rza.at[u, s - 2])
            add(u, o, rza, s - 2)
        send(f"za{u}.{s}", qbuf.at[u, x, zi(o)], rza.at[u, s - 1], dev_a)

    def rb(u, s):
        o = -(4 - s)
        take_x(u, o)
        if s > 1:
            wait(f"zb{u}.{s - 1}", rzb.at[u, s - 2])
            add(u, o, rzb, s - 2)
        send(f"zb{u}.{s}", qbuf.at[u, x, zi(o)], rzb.at[u, s - 1], dev_b)

    def rpa_(u, s):
        wait(f"ha{u}.{s}", rpa.at[u, s - 1])
        o = 3 - s
        addh(u, o, rpa, s - 1)
        if s < 3:
            send(f"ha{u}.{s + 1}", qbuf.at[u, xo, zi(o), :, HI], rpa.at[u, s], dev_a)

    def rpb_(u, s):
        wait(f"hb{u}.{s}", rpb.at[u, s - 1])
        o = -(4 - s)
        addh(u, o, rpb, s - 1)
        if s < 4:
            send(f"hb{u}.{s + 1}", qbuf.at[u, xo, zi(o), :, HI], rpb.at[u, s], dev_b)

    def rpf(u, s):
        rpa_(u, 3)
        rpb_(u, 4)
        send(f"xf{u}", qbuf.at[u, xo, z, :, HI], rxf.at[u], dev_x)

    def drain():
        for c, same in moves:

            @pl.when(jnp.logical_not(same))
            def _():
                c.wait_send()

        moves.clear()

    def fin(u, s):
        if u == 2:
            drain()
        take_x(u, 0)
        wait(f"zb{u}.3", rzb.at[u, 2])
        wait(f"za{u}.4", rza.at[u, 3])
        wait(f"xf{u}", rxf.at[u])
        v = qbuf[u, x, z] + rza[u, 3] + rzb[u, 2]
        g1_out[u, :, LO] = v[:, :KR]
        g1_out[u, :, HI] = v[:, KR:] + rxf[u]
        wait(f"ch{u}", ch.at[u])
        for h in range(2):
            c1_out[u, :, pl.ds(h * KR, KR)] = ch[u, h]

    for u in range(U):
        for i in range(2):
            sem(f"a{u}.{i}")
        for i in range(2):
            sem(f"c{u}.{i}")

    stages = dict(
        ag0=ag0, ga=ga, gb=gb, gx=gx, gpa=gpa, gpb=gpb, mm=mm, ry=ry, xhi=xhi, ay1=ay1, ay2=ay2,
        mmt=mmt, ra=ra, rb=rb, rpa=rpa_, rpb=rpb_, rpf=rpf, fin=fin, hs=hs_, rel=rel, rel2=rel2, crel0=crel0, crel=crel,
    )
    pl.semaphore_wait(barrier, expected)
    ag0(0, 0)
    loads[4].wait()
    send("h", h_ref, hbuf.at[k], dev_core)
    split_rows(k)
    for name, u, s in ORDER:
        stages[name](u, s)
    for u in range(U):
        assert sent[u] == math.prod(tally.shape), sent
        pltpu.make_async_copy(tally, tally, bulk.at[u]).wait()
    pltpu.make_async_copy(h_ref, hbuf.at[k], bulk.at[U]).wait()
    drain()
    assert len(names) <= NSEM, len(names)


NSEM = 320


def run_kernel(h, *arrays):
    v = pltpu.VMEM
    scratch = [
        v((U, 8, KC), F32), v((U, 8, KC), F32), v((U, 8, KC), F32), v((U, 8, KC), jnp.int32),
        v((U, 8, KC), F32), v((U, 8, KC), F32),
        v((2, 448, KC), F32), v((KR, KC), BF16), v((KR, KC), BF16), v((U, 256, KC), BF16),
        v((U, 2, 8, 8, KC), F32),
        v((U, 2, 8, 8, KR), F32),
        v((U, 2, 4, 8, KR), F32), v((U, 2, 2, 8, KR), F32),
        v((U, 2, 2, 8, KR), F32), v((U, 2, 2, 8, KR), F32),
        v((U, 2, 8, 8, KR), F32), v((U, 256, KR), BF16),
        v((U, 2, 8, 8, KC), F32),
        v((U, 8, 8, KR), F32),
        v((U, 4, 8, KC), F32), v((U, 3, 8, KC), F32),
        v((U, 3, 8, KR), F32), v((U, 4, 8, KR), F32),
        v((U, 8, KR), F32),
        v((U, 2, 8, KR), F32), v((U, 2, 8, KR), F32),
        v((U, 8, KC), F32), v((U, 2, 8, KR), F32),
        v((44, 8, KC), F32),
        pltpu.SemaphoreType.DMA((NSEM,)), pltpu.SemaphoreType.DMA((NSEM,)),
        pltpu.SemaphoreType.DMA((5,)), pltpu.SemaphoreType.DMA((U + 1,)),
    ]
    return pl.pallas_call(
        kernel,
        out_shape=[jax.ShapeDtypeStruct((U, 8, KC), F32)] * 2,
        in_specs=[pl.BlockSpec(memory_space=pl.ANY)] * 5,
        out_specs=[pl.BlockSpec(memory_space=pltpu.VMEM)] * 2,
        scratch_shapes=scratch,
        compiler_params=pltpu.CompilerParams(
            collective_id=0, has_side_effects=True, vmem_limit_bytes=56 * 1024 * 1024
        ),
    )(h, *(t.reshape(U, 8, KC) for t in arrays))


def per_device(hessian, dense_weight, start_iterate, start_multiplier, keep_mask):
    weight, iterate0, multiplier0 = dense_weight.T, start_iterate.T, start_multiplier.T
    keeping = keep_mask.T.astype(F32)
    c1, g1 = run_kernel(hessian, weight, iterate0, multiplier0, keep_mask.T)
    iterate1 = c1.reshape(32, KC) + weight
    projected1 = keeping * (iterate1 + multiplier0)
    multiplier1 = multiplier0 + iterate1 - projected1
    iterate2 = iterate1 - STEP * (g1.reshape(32, KC) + (iterate1 - projected1 + multiplier1))
    projected2 = keeping * (iterate2 + multiplier1)
    multiplier2 = multiplier1 + iterate2 - projected2
    return iterate2.T, projected2.T, multiplier2.T


def solution(mesh):
    return jax.shard_map(
        per_device,
        mesh=mesh,
        in_specs=(P("row", "col"),) + (P("col", "row"),) * 4,
        out_specs=(P("col", "row"),) * 3,
        check_vma=False,
    )
```
